32 devices in a mesh: gx: 8 (over z, core), gy: 4 (over y, x).
Axes of the slice: x: 2, y: 2, z: 4, core: 2. Of those that a mesh axis runs over, the one named last changes fastest.
Arguments:
- coarse: bfloat16 [32, 8, 64, 128], P(None, None, 'gy'), may hold values from -6 to 6
- w_three: bfloat16 [27, 16, 32], replicated, may hold values from -0.5 to 0.5
- w_four: bfloat16 [27, 16], replicated, may hold values from -0.75 to 0.75
- elec_field: bfloat16 [3, 32, 256, 512], P(None, 'gx', 'gy'), may hold values from -6 to 6
- temp_grad: bfloat16 [3, 32, 256, 512], P(None, 'gx', 'gy'), may hold values from -6 to 6
- adjoint: bfloat16 [32, 256, 512], P('gx', 'gy'), may hold values from -6 to 6
- adjoint_grad: bfloat16 [3, 32, 256, 512], P(None, 'gx', 'gy'), may hold values from -6 to 6
Outputs:
- density: float32 [32, 256, 512], P('gx', 'gy')
- grad_three: float32 [27, 16, 32], replicated
- grad_four: float32 [27, 16], replicated
The draws below stay inside these ranges and needn't reach their ends.
All inputs are finite; a program needn't handle non-finite values.
Results may differ from the reference program's by a relative error of at most 0.0053.
Values may be sent and summed in bfloat16 or wider, within the bound.
No kernel may reach another device: no remote copies, remote signals or barrier semaphores. Data moves between devices by JAX's collectives and lax.ppermute only.
A program may use at most 128 MiB of HBM per device.

```python
import math
import jax
import jax.numpy as jnp
import numpy as np
from jax import lax

C2 = 32
C3 = 16
NZ = 512
NX = 32
NY = 256


def block_scale(rng, shape, shards, low, high):
    gain, own = 1.0, jax.random.fold_in(rng, 6)
    for axis_at, shards_of in shards:
        steps = jnp.exp(jax.random.uniform(jax.random.fold_in(own, axis_at), (shards_of,), jnp.float32, low / len(shards), high / len(shards)))
        gain = gain * jnp.repeat(steps, shape[axis_at] // shards_of).reshape([-1 if axis == axis_at else 1 for axis in range(len(shape))])
    return gain


def gaussian(own_key, extent, width, most, shards=(), held_as=jnp.bfloat16):
    values = jax.random.normal(own_key, extent, jnp.float32) * width
    if len(shards) > 0:
        values = block_scale(own_key, extent, shards, -0.22, 0.18) * values
    return jnp.clip(values, min=-most, max=most).astype(held_as)


def setup_inputs(seed: int = 0) -> dict:
    keys = jax.random.split(jax.random.key(seed), 8)
    return {
        "coarse": gaussian(keys[0], (C2, NX // 4, NY // 4, NZ // 4), 1.0, 6.0, ((2, 4),)),
        "w_three": gaussian(keys[1], (27, C3, C2), (4 * C2) ** -0.5, 0.5),
        "w_four": gaussian(keys[2], (27, C3), (4 * C3) ** -0.5, 0.75),
        "elec_field": gaussian(keys[3], (3, NX, NY, NZ), 1.0, 6.0, ((1, 8), (2, 4))),
        "temp_grad": gaussian(keys[4], (3, NX, NY, NZ), 1.0, 6.0, ((1, 8), (2, 4))),
        "adjoint": gaussian(keys[5], (NX, NY, NZ), 1.0, 6.0, ((0, 8), (1, 4))),
        "adjoint_grad": gaussian(keys[6], (3, NX, NY, NZ), 1.0, 6.0, ((1, 8), (2, 4))),
    }


HIGH = lax.Precision.HIGHEST

def tap_tables(axis_order):
    strides = (9, 3, 1)
    onehot = np.zeros((8, 8, 27), np.float32)
    for offset in range(8):
        for parity in range(8):
            kernel = 0
            usable = True
            for axis_pos in range(3):
                bit_off = offset >> 2 - axis_pos & 1
                bit_par = parity >> 2 - axis_pos & 1
                if bit_off > bit_par:
                    usable = False
                if bit_par == 0:
                    along = 1
                elif bit_off == 0:
                    along = 2
                else:
                    along = 0
                kernel = kernel + along * strides[axis_order[axis_pos]]
            if usable:
                onehot[offset, parity, kernel] = 1.0
    return onehot

def bits_of(offset):
    return (offset >> 2 & 1, offset >> 1 & 1, offset & 1)

def spread_weight(weight, axis_order):
    lookup = jnp.asarray(tap_tables(axis_order), jnp.float32)
    return jnp.einsum('spk,kqc->spqc', lookup, weight.astype(jnp.float32), precision=HIGH)

def upsample(extended, scatter_outward):
    count_a, count_b, count_c = (extended.shape[1] - 1, extended.shape[2] - 1, extended.shape[3] - 1)
    summed = jnp.zeros((8, scatter_outward.shape[2], count_a, count_b, count_c), jnp.float32)
    for offset in range(8):
        bit_a, bit_b, bit_c = bits_of(offset)
        window = extended[:, bit_a:bit_a + count_a, bit_b:bit_b + count_b, bit_c:bit_c + count_c]
        summed = summed + jnp.einsum('pqc,cabd->pqabd', scatter_outward[offset], window, precision=HIGH)
    return summed

def alternate(summed):
    chans, count_a, count_b, count_c = summed.shape[1:]
    return summed.reshape(2, 2, 2, chans, count_a, count_b, count_c).transpose(3, 4, 0, 5, 1, 6, 2).reshape(chans, 2 * count_a, 2 * count_b, 2 * count_c)

def separate_parity_planes(fine):
    chans, size_a, size_b, size_c = fine.shape
    return fine.reshape(chans, size_a // 2, 2, size_b // 2, 2, size_c // 2, 2).transpose(2, 4, 6, 0, 1, 3, 5).reshape(8, chans, size_a // 2, size_b // 2, size_c // 2)

def weight_terms(extended, parities):
    count_a, count_b, count_c = parities.shape[2:]
    stacked = []
    for offset in range(8):
        bit_a, bit_b, bit_c = bits_of(offset)
        window = extended[:, bit_a:bit_a + count_a, bit_b:bit_b + count_b, bit_c:bit_c + count_c]
        stacked.append(jnp.einsum('pqabd,cabd->pqc', parities, window, precision=HIGH))
    return jnp.stack(stacked)

def fold_taps(terms, axis_order):
    lookup = jnp.asarray(tap_tables(axis_order), jnp.float32)
    return jnp.einsum('spk,spqc->kqc', lookup, terms, precision=HIGH)

def coarsen_resolution(lower_extension, scatter_outward):
    count_a, count_b, count_c = (lower_extension.shape[2] - 1, lower_extension.shape[3] - 1, lower_extension.shape[4] - 1)
    summed = jnp.zeros((scatter_outward.shape[3], count_a, count_b, count_c), jnp.float32)
    for offset in range(8):
        bit_a, bit_b, bit_c = bits_of(offset)
        window = lower_extension[:, :, 1 - bit_a:1 - bit_a + count_a, 1 - bit_b:1 - bit_b + count_b, 1 - bit_c:1 - bit_c + count_c]
        summed = summed + jnp.einsum('pqc,pqabd->cabd', scatter_outward[offset], window, precision=HIGH)
    return summed

def natural_order(field):
    shape = field.shape
    return jnp.swapaxes(field.reshape(shape[:-1] + (4, shape[-1] // 4)), -1, -2).reshape(shape)

def stored_order(field):
    shape = field.shape
    return jnp.swapaxes(field.reshape(shape[:-1] + (shape[-1] // 4, 4)), -1, -2).reshape(shape)

def reference(coarse, w_three, w_four, elec_field, temp_grad, adjoint, adjoint_grad):
    coarse_xyz = coarse.astype(jnp.float32)
    ext_three = jnp.pad(coarse_xyz, ((0, 0), (0, 1), (0, 1), (0, 1)))
    spread_three = spread_weight(w_three, (0, 1, 2))
    pre_three = alternate(upsample(ext_three, spread_three))
    hidden = jax.nn.silu(pre_three).astype(jnp.bfloat16)
    ext_four = jnp.pad(hidden.astype(jnp.float32), ((0, 0), (0, 1), (0, 1), (0, 1)))
    scatter_fourfold = spread_weight(w_four[:, None, :], (0, 1, 2))
    out_four = alternate(upsample(ext_four, scatter_fourfold))[0]
    density = jax.nn.sigmoid(out_four)
    field_e = natural_order(elec_field.astype(jnp.float32))
    energy = lax.optimization_barrier(jnp.sum(field_e * field_e, axis=0))
    thermal = lax.optimization_barrier(jnp.sum(natural_order(temp_grad.astype(jnp.float32)) * natural_order(adjoint_grad.astype(jnp.float32)), axis=0))
    adjoint_f = natural_order(adjoint.astype(jnp.float32))
    sensitivity = 3.0 * (1.0 - 0.001) * density * density * energy * adjoint_f - 2.0 * (1.0 - 0.01) * density * thermal
    scale = 8.0 / math.sqrt(NX * NY * NZ)
    g_out = (scale * sensitivity * density * (1.0 - density)).astype(jnp.bfloat16)
    g_fine = g_out[None].astype(jnp.float32)
    grad_four = fold_taps(weight_terms(ext_four, separate_parity_planes(g_fine)), (0, 1, 2))[:, 0, :]
    lower_extension = jnp.pad(g_fine, ((0, 0), (2, 0), (2, 0), (2, 0)))
    hidden_gradient = coarsen_resolution(separate_parity_planes(lower_extension), scatter_fourfold).astype(jnp.bfloat16)
    sigma_pre = jax.nn.sigmoid(pre_three)
    g_pre = (hidden_gradient.astype(jnp.float32) * sigma_pre * (1.0 + pre_three * (1.0 - sigma_pre))).astype(jnp.bfloat16)
    grad_three = fold_taps(weight_terms(ext_three, separate_parity_planes(g_pre.astype(jnp.float32))), (0, 1, 2))
    return (stored_order(density), grad_three, grad_four)
```

```python
import math

import jax
import jax.numpy as jnp
import numpy as np
from jax import lax
from jax.sharding import PartitionSpec as P

HIGH = lax.Precision.HIGHEST


def passed_along(value, axis, by):
    size = lax.axis_size(axis)
    pairs = [(i, i + by) for i in range(size) if 0 <= i + by < size]
    return lax.ppermute(value, axis, pairs)


def tap_tables():
    onehot = np.zeros((8, 8, 27), np.float32)
    strides = (9, 3, 1)
    for offset in range(8):
        for parity in range(8):
            kernel = 0
            usable = True
            for axis_pos in range(3):
                bit_off = offset >> 2 - axis_pos & 1
                bit_par = parity >> 2 - axis_pos & 1
                if bit_off > bit_par:
                    usable = False
                if bit_par == 0:
                    along = 1
                elif bit_off == 0:
                    along = 2
                else:
                    along = 0
                kernel = kernel + along * strides[axis_pos]
            if usable:
                onehot[offset, parity, kernel] = 1.0
    return onehot


def residue_table():
    per_axis = ({0: 1}, {0: 2, 1: 0}, {1: 1}, {1: 2, 2: 0})
    lookup = np.zeros((64, 27, 27), np.float32)
    for residue in range(64):
        res_x, res_y, res_z = (residue // 16, residue // 4 % 4, residue % 4)
        for src_x, tap_x in per_axis[res_x].items():
            for src_y, tap_y in per_axis[res_y].items():
                for src_z, tap_z in per_axis[res_z].items():
                    lookup[
                        residue, 9 * src_x + 3 * src_y + src_z, 9 * tap_x + 3 * tap_y + tap_z
                    ] = 1.0
    return lookup


def bits_of(offset):
    return (offset >> 2 & 1, offset >> 1 & 1, offset & 1)


def shift_last(block):
    return jnp.concatenate([block[..., 1:], jnp.zeros_like(block[..., :1])], -1)


def delay_last(block):
    return jnp.concatenate([jnp.zeros_like(block[..., :1]), block[..., :-1]], -1)


def beside_y(block, steps_by):
    return passed_along(block, "gy", steps_by)


def silu_slope(values):
    sigma_pre = jax.nn.sigmoid(values)
    return sigma_pre * (1.0 + values * (1.0 - sigma_pre))


def coarse_windows(ext_three, count_a, count_b):
    stacked = []
    for offset in range(8):
        bit_a, bit_b, bit_c = bits_of(offset)
        window = ext_three[:, bit_a : bit_a + count_a, bit_b : bit_b + count_b, :]
        if bit_c == 1:
            window = shift_last(window)
        stacked.append(window)
    merged = jnp.stack(stacked)
    return merged.reshape((merged.shape[0] * merged.shape[1],) + merged.shape[2:])


def layer_three_matrix(weight):
    lookup = jnp.asarray(tap_tables(), jnp.bfloat16)
    spread = jnp.einsum("spk,koc->posc", lookup, weight, preferred_element_type=jnp.float32).astype(
        jnp.bfloat16
    )
    return spread.reshape(8 * weight.shape[1], 8 * weight.shape[2])


def layer_four_matrix(w_four):
    lookup = jnp.asarray(residue_table(), jnp.bfloat16)
    spread = jnp.einsum("usk,ki->usi", lookup, w_four, preferred_element_type=jnp.float32).astype(
        jnp.bfloat16
    )
    return spread.reshape(64, 27 * w_four.shape[1])


def hidden_windows(hidden):
    even_x = hidden[0]
    rim_plane = passed_along(even_x, "gx", -1)
    next_x = jnp.concatenate([even_x[:, :, :, 1:], rim_plane], 3)
    along_x = jnp.stack([even_x, hidden[1], next_x])
    even_y = along_x[:, 0]
    rim_side = beside_y(even_y[:, :, :, :, :1], -1)
    next_y = jnp.concatenate([even_y[:, :, :, :, 1:], rim_side], 4)
    along_y = jnp.stack([even_y, along_x[:, 1], next_y], 1)
    even_z = along_y[:, :, 0]
    along_z = jnp.stack([even_z, along_y[:, :, 1], shift_last(even_z)], 2)
    shape = along_z.shape
    return along_z.reshape((27 * shape[3],) + shape[4:])


def gather_back(spread):
    fold_z = jnp.stack([spread[:, :, 0] + delay_last(spread[:, :, 2]), spread[:, :, 1]], 2)
    later_y = fold_z[:, 2]
    rim_side = passed_along(later_y[:, :, :, :, -1:], "gy", 1)
    moved_y = jnp.concatenate([rim_side, later_y[:, :, :, :, :-1]], 4)
    fold_y = jnp.stack([fold_z[:, 0] + moved_y, fold_z[:, 1]], 1)
    later_x = fold_y[2]
    rim_plane = passed_along(later_x, "gx", 1)
    moved_x = jnp.concatenate([rim_plane, later_x[:, :, :, :-1]], 3)
    fold_x = jnp.stack([fold_y[0] + moved_x, fold_y[1]])
    return fold_x.reshape((8,) + fold_x.shape[3:])


def to_storage(classes, count_a, count_b):
    depth = classes.shape[-1]
    split = classes.reshape(4, 4, 4, count_a, count_b, depth).transpose(3, 0, 4, 1, 2, 5)
    return split.reshape(4 * count_a, 4 * count_b, 4 * depth)


def to_classes(fine, count_a, count_b):
    depth = fine.shape[-1] // 4
    split = fine.reshape(count_a, 4, count_b, 4, 4, depth).transpose(1, 3, 4, 0, 2, 5)
    return split.reshape(64, count_a, count_b, depth)


def first_layer(windows_three, weight):
    matrix_three = layer_three_matrix(weight)
    pre_three = jnp.einsum(
        "qk,kabd->qabd", matrix_three, windows_three, preferred_element_type=jnp.float32
    )
    return pre_three.reshape((8, weight.shape[1]) + pre_three.shape[1:])


def three_gradient(g_pre, windows_three):
    chan_out = g_pre.shape[1]
    flat = g_pre.reshape((8 * chan_out,) + g_pre.shape[2:])
    terms = jnp.einsum("qabd,kabd->qk", flat, windows_three, preferred_element_type=jnp.float32)
    chan_in = windows_three.shape[0] // 8
    terms = terms.reshape(8, chan_out, 8, chan_in)
    lookup = jnp.asarray(tap_tables(), jnp.float32)
    return jnp.einsum("spk,posc->koc", lookup, terms, precision=HIGH)


def exchanged(value, axis, bit):
    size = lax.axis_size(axis)
    return lax.ppermute(value, axis, [(i, i ^ bit) for i in range(size)])


def doubling_bits(size, first):
    bits = []
    bit = first
    while bit < size:
        bits.append(bit)
        bit = bit * 2
    return bits


def sum_halves(half):
    for bit in doubling_bits(lax.axis_size("gx"), 2):
        half = half + exchanged(half, "gx", bit)
    for bit in doubling_bits(lax.axis_size("gy"), 1):
        half = half + exchanged(half, "gy", bit)
    return half


def sum_everywhere(grad_three, grad_four):
    for axis in ("gx", "gy"):
        size = lax.axis_size(axis)
        assert size & (size - 1) == 0
    flat = jnp.concatenate([grad_three.reshape(-1), grad_four.reshape(-1)])
    held = flat.shape[0]
    rows = -(-held // 2048) * 16
    packed = jnp.pad(flat, (0, rows * 128 - held)).reshape(2, rows // 2, 128)
    core = lax.axis_index("gx") % 2
    mine = jnp.where(core == 0, packed[0], packed[1])
    other = jnp.where(core == 0, packed[1], packed[0])
    mine = sum_halves(mine + exchanged(other, "gx", 1))
    other = exchanged(mine, "gx", 1)
    first = jnp.where(core == 0, mine, other)
    second = jnp.where(core == 0, other, mine)
    summed = jnp.concatenate([first, second]).reshape(-1)
    count_three = grad_three.size
    return (
        summed[:count_three].reshape(grad_three.shape),
        summed[count_three:held].reshape(grad_four.shape),
    )


def shards(coarse, w_three, w_four, elec_field, temp_grad, adjoint, adjoint_grad):
    groups_x = lax.axis_size("gx")
    chan_total, chan_in = (w_three.shape[1], w_three.shape[2])
    fine_x, fine_y, fine_z = adjoint.shape
    count_a, count_b = (fine_x // 4, fine_y // 4)
    cells = fine_x * groups_x * fine_y * lax.axis_size("gy") * fine_z
    rim_row = beside_y(coarse[:, :, :1], -1)
    ext_full = jnp.pad(jnp.concatenate([coarse, rim_row], 2), ((0, 0), (0, 1), (0, 0), (0, 0)))
    ext_brick = lax.dynamic_slice_in_dim(ext_full, lax.axis_index("gx") * count_a, count_a + 1, 1)
    windows_three = coarse_windows(ext_brick, count_a, count_b)
    pre_three = first_layer(windows_three, w_three)
    hidden = jax.nn.silu(pre_three).astype(jnp.bfloat16)
    hidden = hidden.reshape((2, 2, 2) + hidden.shape[1:])
    windows_four = hidden_windows(hidden)
    matrix_four = layer_four_matrix(w_four)
    out_four = jnp.einsum(
        "qk,kabd->qabd", matrix_four, windows_four, preferred_element_type=jnp.float32
    )
    density = to_storage(jax.nn.sigmoid(out_four), count_a, count_b)
    field_e = elec_field.astype(jnp.float32)
    energy = jnp.sum(field_e * field_e, axis=0)
    thermal = jnp.sum(temp_grad.astype(jnp.float32) * adjoint_grad.astype(jnp.float32), axis=0)
    adjoint_f = adjoint.astype(jnp.float32)
    sensitivity = (
        3.0 * (1.0 - 0.001) * density * density * energy * adjoint_f
        - 2.0 * (1.0 - 0.01) * density * thermal
    )
    scale = 8.0 / math.sqrt(cells)
    g_fine = (scale * sensitivity * density * (1.0 - density)).astype(jnp.bfloat16)
    g_classes = to_classes(g_fine, count_a, count_b)
    terms_four = jnp.einsum(
        "qabd,kabd->qk", g_classes, windows_four, preferred_element_type=jnp.float32
    )
    grad_four = jnp.einsum(
        "usk,usi->ki",
        jnp.asarray(residue_table(), jnp.float32),
        terms_four.reshape(64, 27, chan_total),
        precision=HIGH,
    )
    spread_back = jnp.einsum(
        "qk,qabd->kabd", matrix_four, g_classes, preferred_element_type=jnp.float32
    )
    spread_back = spread_back.reshape((3, 3, 3, chan_total) + spread_back.shape[1:])
    hidden_gradient = gather_back(spread_back).astype(jnp.bfloat16)
    g_pre = (hidden_gradient.astype(jnp.float32) * silu_slope(pre_three)).astype(jnp.bfloat16)
    grad_three = three_gradient(g_pre, windows_three)
    grad_three, grad_four = sum_everywhere(grad_three, grad_four)
    return (density, grad_three, grad_four)


def solution(mesh):
    return jax.shard_map(
        shards,
        mesh=mesh,
        in_specs=(
            P(None, None, "gy", None),
            P(),
            P(),
            P(None, "gx", "gy", None),
            P(None, "gx", "gy", None),
            P("gx", "gy", None),
            P(None, "gx", "gy", None),
        ),
        out_specs=(P("gx", "gy", None), P(), P()),
        check_vma=False,
    )
```

```python
import math

import jax
import jax.numpy as jnp
import numpy as np
from jax import lax
from jax.experimental import pallas as pl
from jax.experimental.pallas import tpu as pltpu
from jax.sharding import PartitionSpec as P

ROWS = 4
HIDDEN_ROWS = 2 * ROWS + 1
PAIR_ROWS = 5
BLOCKS = 3 * PAIR_ROWS * 3
LANES = 128
MIB = 1024 * 1024


def axis_tap(parity, offset):
    if parity == 0:
        return 1
    return 2 if offset == 0 else 0


def block_taps():
    per_axis = ({0: 1}, {0: 2, 1: 0}, {1: 1}, {1: 2, 2: 0})
    table = np.full((48, LANES), -1, np.int32)
    for src_x in range(3):
        for src_y in range(PAIR_ROWS):
            for src_z in range(3):
                block = (src_x * PAIR_ROWS + src_y) * 3 + src_z
                for res_x in range(4):
                    for res_z in range(4):
                        for row in range(8):
                            along_y = src_y - 2 * (row // 4)
                            tap_x = per_axis[res_x].get(src_x)
                            tap_y = per_axis[row % 4].get(along_y)
                            tap_z = per_axis[res_z].get(src_z)
                            if tap_x is None or tap_y is None or tap_z is None:
                                continue
                            at = (res_x * 4 + res_z) * 8 + row
                            table[block, at] = 9 * tap_x + 3 * tap_y + tap_z
    return table


def slot_of(tap):
    tap_x, tap_y, tap_z = (tap // 9, tap // 3 % 3, tap % 3)
    off_y, off_z = (int(tap_y == 0), int(tap_z == 0))
    if tap_y == 1 and tap_z == 1:
        return (96, 32 * tap_x)
    if tap_y == 1:
        return (32 * tap_x + 16, 32 * off_z)
    if tap_z == 1:
        return (32 * tap_x + 16, 64 if off_y == 1 else 96)
    return (32 * tap_x, 64 * off_y + 32 * off_z)


def lane_index(shape):
    return lax.broadcasted_iota(jnp.int32, shape, 1)


def next_lane(tile):
    moved = pltpu.roll(tile, LANES - 1, 1)
    return jnp.where(lane_index(tile.shape) == LANES - 1, 0.0, moved)


def previous_lane(tile):
    moved = pltpu.roll(tile, 1, 1)
    return jnp.where(lane_index(tile.shape) == 0, 0.0, moved)


def logistic(values):
    return 1.0 / (1.0 + jnp.exp(-values))


def matmul(left, right):
    return jnp.dot(left, right, preferred_element_type=jnp.float32)


def matmul_nt(left, right):
    return lax.dot_general(
        left, right, (((1,), (1,)), ((), ())), preferred_element_type=jnp.float32
    )


def fill_onehot(taps, onehot):
    row = lax.broadcasted_iota(jnp.int32, (32, LANES), 0)
    for block in range(BLOCKS):
        hit = row == jnp.broadcast_to(taps[block : block + 1, :], (32, LANES))
        onehot[:, block * LANES : (block + 1) * LANES] = jnp.where(hit, 1.0, 0.0).astype(
            jnp.bfloat16
        )


def fill_matrices(w_three, w_four, onehot, m_three, m_four, m_back, build):
    build[...] = jnp.zeros_like(build)
    for tap in range(27):
        tap_x, tap_y, tap_z = (tap // 9, tap // 3 % 3, tap % 3)
        par_y, off_y = (int(tap_y != 1), int(tap_y == 0))
        par_z, off_z = (int(tap_z != 1), int(tap_z == 0))
        row = par_y * 32 + par_z * 16
        lane = off_y * 64 + off_z * 32
        places = (((1, 1),), ((0, 0), (2, 1)), ((1, 0),))[tap_x]
        values = w_three[tap].astype(jnp.float32)
        for plane, off_x in places:
            build[
                plane * 64 + row : plane * 64 + row + 16,
                off_x * 128 + lane : off_x * 128 + lane + 32,
            ] = values
    m_three[...] = build[...].astype(jnp.bfloat16)
    spread = matmul(w_four[...], onehot[:27, :])
    columns = jnp.concatenate(
        [spread[:, block * LANES : (block + 1) * LANES] for block in range(BLOCKS)], 0
    )
    m_back[...] = columns.astype(jnp.bfloat16)
    m_four[...] = columns.T.astype(jnp.bfloat16)


def coarse_tile(rows):
    return jnp.concatenate([rows, next_lane(rows)], 0).astype(jnp.bfloat16)


def field_pair(elec, temp, adj, adj_grad, scale, res_x, lanes):
    energy = 0.0
    thermal = 0.0
    for comp in range(3):
        field = elec[comp, res_x, :, lanes].astype(jnp.float32)
        energy = energy + field * field
        thermal = thermal + temp[comp, res_x, :, lanes].astype(jnp.float32) * adj_grad[
            comp, res_x, :, lanes
        ].astype(jnp.float32)
    gain = (scale * 3.0 * (1.0 - 0.001)) * (energy * adj[res_x, :, lanes].astype(jnp.float32))
    return (gain, (scale * 2.0 * (1.0 - 0.01)) * thermal)


def quad(refs, tiles, field_terms):
    (m_three, m_four, m_back, density) = refs[:4]
    (sum_three, sum_four, wide, slope, windows, g_fine, g_pre) = refs[4:]
    blank = jnp.zeros((64, LANES), jnp.bfloat16)
    for b in range(ROWS + 1):
        for plane in range(2):
            after = tiles[plane][b + 1] if b < ROWS else blank
            wide[plane * 128 : plane * 128 + 64, b * LANES : (b + 1) * LANES] = tiles[plane][b]
            wide[plane * 128 + 64 : plane * 128 + 128, b * LANES : (b + 1) * LANES] = after
    pre = matmul(m_three[...], wide[...])
    sigma = logistic(pre)
    hidden = pre * sigma
    slope[...] = sigma * (1.0 + pre * (1.0 - sigma))
    for plane in range(3):
        for row in range(HIDDEN_ROWS):
            b, par = (row // 2, row % 2)
            at = plane * 64 + par * 32
            both = hidden[at : at + 32, b * LANES : (b + 1) * LANES]
            tall = jnp.concatenate([both, next_lane(both[:16])], 0).astype(jnp.bfloat16)
            for half in range(2):
                within = row - 4 * half
                if 0 <= within < PAIR_ROWS:
                    start = (plane * PAIR_ROWS + within) * 48
                    windows[start : start + 48, half * LANES : (half + 1) * LANES] = tall
    dens = logistic(matmul(m_four[...], windows[...]))
    for res_x in range(4):
        for res_z in range(4):
            at = (res_x * 4 + res_z) * 8
            lanes = slice(res_z * LANES, (res_z + 1) * LANES)
            d = jnp.concatenate([dens[at : at + 8, :LANES], dens[at : at + 8, LANES:]], 0)
            density[res_x, :, lanes] = d
            gain, loss = field_terms(res_x, lanes)
            g = d * d * (1.0 - d) * (gain * d - loss)
            g_fine[at : at + 8, :LANES] = g[:8]
            g_fine[at : at + 8, LANES:] = g[8:]
    g_out = g_fine[...].astype(jnp.bfloat16)
    sum_four[...] += matmul_nt(windows[...], g_out)
    spread = matmul(m_back[...], g_out)
    for plane in range(3):
        for row in range(HIDDEN_ROWS):
            b, par = (row // 2, row % 2)
            tall = 0.0
            for half in range(2):
                within = row - 4 * half
                if 0 <= within < PAIR_ROWS:
                    start = (plane * PAIR_ROWS + within) * 48
                    tall = tall + spread[start : start + 48, half * LANES : (half + 1) * LANES]
            both = jnp.concatenate([tall[:16] + previous_lane(tall[32:]), tall[16:32]], 0)
            at = plane * 64 + par * 32
            lanes = slice(b * LANES, (b + 1) * LANES)
            if plane == 1 and 0 < row < HIDDEN_ROWS - 1:
                both = both.astype(jnp.bfloat16).astype(jnp.float32)
            g_pre[at : at + 32, lanes] = (both * slope[at : at + 32, lanes]).astype(jnp.bfloat16)
        g_pre[plane * 64 + 32 : plane * 64 + 64, ROWS * LANES :] = jnp.zeros(
            (32, LANES), jnp.bfloat16
        )
    sum_three[...] += matmul_nt(g_pre[...], wide[...])


def interior_kernel(scale, count_a, place, *refs):
    (near, far, w_three, w_four, taps, elec, temp, adj, adj_grad) = refs[:9]
    (density, sum_three, sum_four, m_three, m_four, m_back) = refs[9:15]
    (last_gain, last_loss, last_cells) = refs[15:18]
    (build, onehot, flat, cells, wide, slope, windows, g_fine, g_pre) = refs[18:]
    step = pl.program_id(0)
    held = near.shape[2]

    @pl.when(step == 0)
    def _():
        sum_three[...] = jnp.zeros_like(sum_three)
        sum_four[...] = jnp.zeros_like(sum_four)
        fill_onehot(taps, onehot)
        fill_matrices(w_three, w_four, onehot, m_three, m_four, m_back, build)
        inside = (place[0] + 1 < count_a).astype(jnp.float32)
        for plane, block in enumerate((near, far)):
            values = block[:, 0].astype(jnp.float32)
            if plane == 1:
                values = values * inside
            flat[plane] = values.reshape(flat.shape[1:])
        for plane in range(2):
            for b in range(held):
                tile = coarse_tile(flat[plane, pl.ds(b, 32, held), :])
                cells[plane, b] = tile
                if b >= held - ROWS:
                    last_cells[plane, b - held + ROWS] = tile

    def field_terms(res_x, lanes):
        return field_pair(elec, temp, adj, adj_grad, scale, res_x, lanes)

    @pl.when(step < pl.num_programs(0) - 1)
    def _():
        tiles = [[cells[plane, step * ROWS + b] for b in range(ROWS + 1)] for plane in range(2)]
        quad(
            (m_three, m_four, m_back, density)
            + (sum_three, sum_four, wide, slope, windows, g_fine, g_pre),
            tiles,
            field_terms,
        )

    @pl.when(step == pl.num_programs(0) - 1)
    def _():
        for res_x in range(4):
            for res_z in range(4):
                lanes = slice(res_z * LANES, (res_z + 1) * LANES)
                gain, loss = field_terms(res_x, lanes)
                last_gain[res_x, :, lanes] = gain
                last_loss[res_x, :, lanes] = loss


def rim_kernel(count_a, place, *refs):
    (rim, taps, m_three, m_four, m_back, sum_three_in, sum_four_in) = refs[:7]
    (last_gain, last_loss, last_cells, _) = refs[7:11]
    (density, mine, other) = refs[11:14]
    (packed, sum_three, sum_four, onehot, wide, slope, windows, g_fine, g_pre) = refs[14:]
    sum_three[...] = sum_three_in[...]
    sum_four[...] = sum_four_in[...]
    inside = (place[0] + 1 < count_a).astype(jnp.float32)
    tiles = []
    for plane in range(2):
        edge = rim[plane].astype(jnp.float32)
        if plane == 1:
            edge = edge * inside
        tiles.append([last_cells[plane, b] for b in range(ROWS)] + [coarse_tile(edge)])
    fill_onehot(taps, onehot)
    quad(
        (m_three, m_four, m_back, density)
        + (sum_three, sum_four, wide, slope, windows, g_fine, g_pre),
        tiles,
        lambda res_x, lanes: (last_gain[res_x, :, lanes], last_loss[res_x, :, lanes]),
    )
    by_tap = (
        sum_three[64:128, 128:],
        sum_three[:64, :128] + sum_three[128:, 128:],
        sum_three[64:128, :128],
    )
    for tap_x in range(3):
        part = by_tap[tap_x]
        packed[32 * tap_x : 32 * tap_x + 16, :] = part[48:64]
        lanes = lane_index((16, LANES))
        mixed = jnp.where(
            lanes < 64,
            part[16:32],
            jnp.where(lanes < 96, part[32:48], pltpu.roll(part[32:48], 96, 1)),
        )
        packed[32 * tap_x + 16 : 32 * tap_x + 32, :] = mixed
        packed[96:112, 32 * tap_x : 32 * tap_x + 32] = part[:16, :32]
    rest = jnp.concatenate(
        [sum_four[16 * block : 16 * block + 16, :] for block in range(BLOCKS)], 1
    )
    pieces = []
    for _ in range(3):
        piece = rest.astype(jnp.bfloat16)
        pieces.append(piece)
        rest = rest - piece.astype(jnp.float32)
    folded = matmul_nt(jnp.concatenate(pieces, 0), onehot[...])
    packed[96:112, 96:128] = folded[:16] + folded[16:32] + folded[32:48]
    part = place[1]
    half = mine.shape[0]
    mine[...] = packed[pl.ds(pl.multiple_of(part * half, 8), half), :]
    other[...] = packed[pl.ds(pl.multiple_of((1 - part) * half, 8), half), :]


def unpack_kernel(part, mine, other, grad_three, grad_four):
    low = part[0] == 0
    whole = jnp.concatenate(
        [
            jnp.where(low, mine[...], other[...]),
            jnp.where(low, other[...], mine[...]),
        ],
        0,
    )
    for tap in range(27):
        row, lane = slot_of(tap)
        grad_three[tap] = whole[row : row + 16, lane : lane + 32]
    grad_four[...] = whole[96:112, 96:123]


def exchanged(value, bit_x, bit_y):
    size_x, size_y = (lax.axis_size("gx"), lax.axis_size("gy"))
    pairs = [
        (i * size_y + j, (i ^ bit_x) * size_y + (j ^ bit_y))
        for i in range(size_x)
        for j in range(size_y)
    ]
    return lax.ppermute(value, ("gx", "gy"), pairs)


def parity_of(index):
    total = index
    for shift in (1, 2, 3, 4, 5, 6, 7):
        total = total ^ (index >> shift)
    return total & 1


def sum_everywhere(mine, other, part):
    size_x, size_y = (lax.axis_size("gx"), lax.axis_size("gy"))
    assert size_x & (size_x - 1) == 0 and size_y & (size_y - 1) == 0
    assert 2 <= size_x <= 256 and size_y <= 256
    mine = mine + exchanged(other, 1, 0)
    bit = 2
    while bit < size_x:
        mine = mine + exchanged(mine, bit + 1, 0)
        bit = bit * 2
    bit = 1
    while bit < size_y:
        mine = mine + exchanged(mine, 1, bit)
        bit = bit * 2
    other = exchanged(mine, 1, 0)
    spec = pl.BlockSpec(memory_space=pltpu.VMEM)
    grad_three, grad_four = pl.pallas_call(
        unpack_kernel,
        out_shape=(
            jax.ShapeDtypeStruct((27, 16, 32), jnp.float32),
            jax.ShapeDtypeStruct((16, 27), jnp.float32),
        ),
        in_specs=[pl.BlockSpec(memory_space=pltpu.SMEM), spec, spec],
        out_specs=(spec, spec),
        compiler_params=pltpu.CompilerParams(vmem_limit_bytes=2 * MIB),
        name="unpack",
    )(part, mine, other)
    return (grad_three, grad_four.T)


def shards(coarse, w_three, w_four, elec_field, temp_grad, adjoint, adjoint_grad):
    groups_x, groups_y = (lax.axis_size("gx"), lax.axis_size("gy"))
    chan_in, count_a, held, depth = coarse.shape
    fine_x, fine_y, fine_z = adjoint.shape
    assert (fine_x, fine_y, fine_z) == (4, 4 * held, 4 * LANES)
    assert depth == LANES and chan_in == 32 and held % ROWS == 0 and count_a == groups_x
    cells = fine_x * groups_x * fine_y * groups_y * fine_z
    scale = 8.0 / math.sqrt(cells)
    at_x = lax.axis_index("gx").astype(jnp.int32)
    far_x = jnp.minimum(at_x + 1, count_a - 1)
    first_row = jnp.concatenate(
        [
            lax.dynamic_slice(coarse, (0, at, 0, 0), (chan_in, 1, 1, depth)).reshape(
                1, chan_in, depth
            )
            for at in (at_x, far_x)
        ],
        0,
    )
    rim = lax.ppermute(first_row, "gy", [(i + 1, i) for i in range(groups_y - 1)])
    part = parity_of(lax.axis_index("gx")) ^ parity_of(lax.axis_index("gy"))
    place = jnp.stack([at_x, part.astype(jnp.int32)])
    taps = jnp.asarray(block_taps())
    steps = held // ROWS
    window_rows = 48 * 3 * PAIR_ROWS
    inner = (
        pltpu.VMEM((256, (ROWS + 1) * LANES), jnp.bfloat16),
        pltpu.VMEM((192, (ROWS + 1) * LANES), jnp.float32),
        pltpu.VMEM((window_rows, 2 * LANES), jnp.bfloat16),
        pltpu.VMEM((LANES, 2 * LANES), jnp.float32),
        pltpu.VMEM((192, (ROWS + 1) * LANES), jnp.bfloat16),
    )
    onehot = pltpu.VMEM((32, BLOCKS * LANES), jnp.bfloat16)

    def whole(entry):
        return pl.BlockSpec(entry.shape, lambda step, place: (0,) * len(entry.shape))

    def shape(dims, dtype):
        return jax.ShapeDtypeStruct(dims, dtype)

    def in_hbm(value):
        return pltpu.with_memory_space_constraint(value, pltpu.HBM)

    triple = pl.BlockSpec((3, 4, 16, fine_z), lambda step, place: (0, 0, step, 0))
    single = pl.BlockSpec((4, 16, fine_z), lambda step, place: (0, step, 0))
    dense = shape(adjoint.shape, jnp.float32)
    sums = (shape((192, 256), jnp.float32), shape((window_rows, LANES), jnp.float32))
    matrices = (
        shape((192, 256), jnp.bfloat16),
        shape((LANES, window_rows), jnp.bfloat16),
        shape((window_rows, LANES), jnp.bfloat16),
    )
    handed = (
        shape((4, 16, fine_z), jnp.float32),
        shape((4, 16, fine_z), jnp.float32),
        shape((2, ROWS, 64, LANES), jnp.bfloat16),
    )
    half = shape((56, LANES), jnp.float32)
    w_four_t = w_four.T
    coarse_hbm = in_hbm(coarse)
    density, sum_three, sum_four, m_three, m_four, m_back, *rest = pl.pallas_call(
        lambda *refs: interior_kernel(scale, count_a, *refs),
        out_shape=(dense,) + sums + matrices + handed,
        grid_spec=pltpu.PrefetchScalarGridSpec(
            num_scalar_prefetch=1,
            grid=(steps,),
            in_specs=[
                pl.BlockSpec((chan_in, 1, held, depth), lambda step, place: (0, place[0], 0, 0)),
                pl.BlockSpec(
                    (chan_in, 1, held, depth),
                    lambda step, place: (0, jnp.minimum(place[0] + 1, count_a - 1), 0, 0),
                ),
                whole(w_three),
                whole(w_four_t),
                whole(taps),
                triple,
                triple,
                single,
                triple,
            ],
            out_specs=[
                pl.BlockSpec(
                    (4, 16, fine_z), lambda step, place: (0, jnp.minimum(step, steps - 2), 0)
                )
            ]
            + [whole(entry) for entry in sums + matrices + handed],
            scratch_shapes=(
                pltpu.VMEM((192, 256), jnp.float32),
                onehot,
                pltpu.VMEM((2, chan_in * held, LANES), jnp.float32),
                pltpu.VMEM((2, held, 64, LANES), jnp.bfloat16),
            )
            + inner,
        ),
        compiler_params=pltpu.CompilerParams(vmem_limit_bytes=24 * MIB),
        cost_estimate=pl.CostEstimate(
            flops=2000000000, bytes_accessed=4000000, transcendentals=2000000
        ),
        name="interior",
    )(
        place,
        coarse_hbm,
        coarse_hbm,
        w_three,
        w_four_t,
        taps,
        in_hbm(elec_field),
        in_hbm(temp_grad),
        in_hbm(adjoint),
        in_hbm(adjoint_grad),
    )
    density, mine, other = pl.pallas_call(
        lambda *refs: rim_kernel(count_a, *refs),
        out_shape=(dense, half, half),
        grid_spec=pltpu.PrefetchScalarGridSpec(
            num_scalar_prefetch=1,
            grid=(1,),
            in_specs=[whole(rim), whole(taps)]
            + [whole(entry) for entry in matrices + sums + handed]
            + [pl.BlockSpec(memory_space=pl.ANY)],
            out_specs=[
                pl.BlockSpec((4, 16, fine_z), lambda step, place: (0, steps - 1, 0)),
                whole(half),
                whole(half),
            ],
            scratch_shapes=(pltpu.VMEM((112, LANES), jnp.float32),)
            + tuple(pltpu.VMEM(entry.shape, entry.dtype) for entry in sums)
            + (onehot,)
            + inner,
        ),
        input_output_aliases={11: 0},
        compiler_params=pltpu.CompilerParams(vmem_limit_bytes=16 * MIB),
        cost_estimate=pl.CostEstimate(
            flops=700000000, bytes_accessed=2000000, transcendentals=700000
        ),
        name="rim",
    )(place, rim, taps, m_three, m_four, m_back, sum_three, sum_four, *rest, density)
    grad_three, grad_four = sum_everywhere(mine, other, place[1:])
    return (density, grad_three, grad_four)


def solution(mesh):
    return jax.shard_map(
        shards,
        mesh=mesh,
        in_specs=(
            P(None, None, "gy", None),
            P(),
            P(),
            P(None, "gx", "gy", None),
            P(None, "gx", "gy", None),
            P("gx", "gy", None),
            P(None, "gx", "gy", None),
        ),
        out_specs=(P("gx", "gy", None), P(), P()),
        check_vma=False,
    )
```

```python
import math

import jax
import jax.numpy as jnp
from jax import lax
from jax.experimental import pallas as pl
from jax.experimental.pallas import tpu as pltpu
from jax.sharding import PartitionSpec as P

PAIR_ROWS = 5
BLOCKS = 3 * PAIR_ROWS * 3
WINDOW = BLOCKS * 16
LANES = 128
MIB = 1024 * 1024


def slot_of(tap):
    tap_x, tap_y, tap_z = (tap // 9, tap // 3 % 3, tap % 3)
    off_y, off_z = (int(tap_y == 0), int(tap_z == 0))
    if tap_y == 1 and tap_z == 1:
        return (96, 32 * tap_x)
    if tap_y == 1:
        return (32 * tap_x + 16, 32 * off_z)
    if tap_z == 1:
        return (32 * tap_x + 16, 64 if off_y == 1 else 96)
    return (32 * tap_x, 64 * off_y + 32 * off_z)


def lane_index(shape):
    return lax.broadcasted_iota(jnp.int32, shape, 1)


def next_lane(tile):
    moved = pltpu.roll(tile, LANES - 1, 1)
    return jnp.where(lane_index(tile.shape) == LANES - 1, 0.0, moved)


def previous_lane(tile):
    moved = pltpu.roll(tile, 1, 1)
    return jnp.where(lane_index(tile.shape) == 0, 0.0, moved)


def logistic(values):
    return 1.0 / (1.0 + jnp.exp(-values))


def matmul(left, right):
    return jnp.dot(left, right, preferred_element_type=jnp.float32)


def matmul_nt(left, right):
    return lax.dot_general(
        left, right, (((1,), (1,)), ((), ())), preferred_element_type=jnp.float32
    )


def block_lanes(block):
    return slice(block * LANES, (block + 1) * LANES)


def fill_onehot(onehot):
    tap = lax.broadcasted_iota(jnp.int32, (32, LANES), 0)
    at = lane_index((32, LANES))
    tap_x = jnp.where(tap >= 9, 1, 0) + jnp.where(tap >= 18, 1, 0)
    within = tap - 9 * tap_x
    tap_y = jnp.where(within >= 3, 1, 0) + jnp.where(within >= 6, 1, 0)
    tap_z = within - 3 * tap_y
    twice_x = (at >> 5) + 1 - tap_x
    twice_z = ((at >> 3) & 3) + 1 - tap_z
    twice_y = (at & 7) + 1 - tap_y
    code = (twice_x + 2) * 256 + (twice_y + 2) * 16 + (twice_z + 2)
    code = jnp.where(tap < 27, code, -1)
    for block in range(BLOCKS):
        src_x, src_y, src_z = (block // 15, block // 3 % 5, block % 3)
        wanted = (2 * src_x + 2) * 256 + (2 * src_y + 2) * 16 + (2 * src_z + 2)
        onehot[:, block_lanes(block)] = jnp.where(code == wanted, 1.0, 0.0).astype(jnp.bfloat16)
        if block % 5 == 4:
            yield


def fill_three(w_three, m_three, build):
    build[...] = jnp.zeros_like(build)
    for tap in range(27):
        tap_x, tap_y, tap_z = (tap // 9, tap // 3 % 3, tap % 3)
        par_y, off_y = (int(tap_y != 1), int(tap_y == 0))
        par_z, off_z = (int(tap_z != 1), int(tap_z == 0))
        row = par_y * 32 + par_z * 16
        lane = off_y * 64 + off_z * 32
        places = (((1, 1),), ((0, 0), (2, 1)), ((1, 0),))[tap_x]
        values = w_three[tap].astype(jnp.float32)
        for plane, off_x in places:
            build[
                plane * 64 + row : plane * 64 + row + 16,
                off_x * 128 + lane : off_x * 128 + lane + 32,
            ] = values
    m_three[...] = build[...].astype(jnp.bfloat16)


def fill_four(w_four, onehot, m_four, m_back):
    spread = matmul(w_four[...], onehot[:27, :])
    columns = jnp.concatenate([spread[:, block_lanes(block)] for block in range(BLOCKS)], 0)
    m_back[...] = columns.astype(jnp.bfloat16)
    m_four[...] = columns.T.astype(jnp.bfloat16)


def coarse_tile(rows):
    return jnp.concatenate([rows, next_lane(rows)], 0).astype(jnp.bfloat16)


def window_of(cells, b, last):
    after = b if last else b + 1
    return jnp.concatenate([cells[0, b], cells[0, after], cells[1, b], cells[1, after]], 0)


def field_pair(elec, temp, adj, adj_grad, scale, res_x, rows, lanes):
    energy = 0.0
    thermal = 0.0
    for comp in range(3):
        field = elec[comp, res_x, rows, lanes].astype(jnp.float32)
        energy = energy + field * field
        thermal = thermal + temp[comp, res_x, rows, lanes].astype(jnp.float32) * adj_grad[
            comp, res_x, rows, lanes
        ].astype(jnp.float32)
    gain = (scale * 3.0 * (1.0 - 0.001)) * (energy * adj[res_x, rows, lanes].astype(jnp.float32))
    return (gain, (scale * 2.0 * (1.0 - 0.01)) * thermal)


class Group:
    def __init__(self, pairs, first, matrices, scratch, top):
        self.pairs, self.first, self.top = (pairs, first, top)
        self.m_three, self.m_four, self.m_back = matrices
        self.cells, self.windows, self.slope, self.g_fine, self.g_pre = scratch
        self.hidden_rows = 4 * pairs + 1

    def window(self, b):
        return window_of(self.cells, self.first + b, self.top and b == 2 * self.pairs)

    def forward(self):
        coarse_rows = 2 * self.pairs + 1
        self.g_pre_blank()
        for b in range(coarse_rows):
            halo = b == coarse_rows - 1
            if halo:
                matrix = jnp.concatenate(
                    [self.m_three[plane * 64 : plane * 64 + 32, :] for plane in range(3)], 0
                )
                part = matmul(matrix, self.window(b))
            elif b % 2 == 0:
                both = matmul(
                    self.m_three[...],
                    jnp.concatenate([self.window(b), self.window(b + 1)], 1),
                )
                part = both[:, :LANES]
            else:
                part = both[:, LANES:]
            per_plane = 32 if halo else 64
            for plane in range(3):
                pre = part[plane * per_plane : (plane + 1) * per_plane]
                sigma = logistic(pre)
                hidden = pre * sigma
                self.slope[plane * 64 : plane * 64 + per_plane, block_lanes(b)] = sigma * (
                    1.0 + pre * (1.0 - sigma)
                )
                for par in range(per_plane // 32):
                    row = 2 * b + par
                    two = hidden[par * 32 : par * 32 + 32]
                    tall = jnp.concatenate([two, next_lane(two[:16])], 0).astype(jnp.bfloat16)
                    for pair in range(self.pairs):
                        within = row - 4 * pair
                        if 0 <= within < PAIR_ROWS:
                            start = (plane * PAIR_ROWS + within) * 48
                            self.windows[start : start + 48, block_lanes(pair)] = tall
                yield

    def g_pre_blank(self):
        for plane in range(3):
            self.g_pre[plane * 64 + 32 : plane * 64 + 64, block_lanes(2 * self.pairs)] = jnp.zeros(
                (32, LANES), jnp.bfloat16
            )

    def backward(self, field_terms, density, sums_from, sums_to):
        logits = matmul(self.m_four[...], self.windows[...])
        for res_x in range(4):
            for res_z in range(4):
                at = (res_x * 4 + res_z) * 8
                lanes = block_lanes(res_z)
                d = logistic(
                    jnp.concatenate(
                        [logits[at : at + 8, block_lanes(pair)] for pair in range(self.pairs)], 0
                    )
                )
                density[res_x, :, lanes] = d
                gain, loss = field_terms(res_x, lanes)
                g = d * d * (1.0 - d) * (gain * d - loss)
                for pair in range(self.pairs):
                    self.g_fine[at : at + 8, block_lanes(pair)] = g[8 * pair : 8 * pair + 8]
            yield
        g_out = self.g_fine[...].astype(jnp.bfloat16)
        for plane in range(3):
            span = slice(plane * 240, plane * 240 + 240)
            spread = matmul(self.m_back[span, :], g_out)
            for row in range(self.hidden_rows):
                tall = 0.0
                for pair in range(self.pairs):
                    within = row - 4 * pair
                    if 0 <= within < PAIR_ROWS:
                        tall = tall + spread[within * 48 : within * 48 + 48, block_lanes(pair)]
                both = jnp.concatenate([tall[:16] + previous_lane(tall[32:]), tall[16:32]], 0)
                at = plane * 64 + row % 2 * 32
                lanes = block_lanes(row // 2)
                if plane == 1 and 0 < row < self.hidden_rows - 1:
                    both = both.astype(jnp.bfloat16).astype(jnp.float32)
                self.g_pre[at : at + 32, lanes] = (
                    both * self.slope[at : at + 32, lanes]
                ).astype(jnp.bfloat16)
            yield
            sums_to[1][span, :] = sums_from[1][span, :] + matmul_nt(self.windows[span, :], g_out)
            yield
        wide = jnp.concatenate([self.window(b) for b in range(2 * self.pairs + 1)], 1)
        sums_to[0][...] = sums_from[0][...] + matmul_nt(self.g_pre[...], wide)
        yield


def run(*streams):
    live = list(streams)
    while live:
        for stream in list(live):
            if next(stream, live) is live:
                live.remove(stream)


def chain(*streams):
    for stream in streams:
        yield from stream


def interior_kernel(scale, near_far, w_three, w_four, elec, temp, adj, adj_grad, *refs):
    (density, sum_three, sum_four, m_three, m_four, m_back) = refs[:6]
    (onehot, last_gain, last_loss, last_cells) = refs[6:10]
    (build, flat, cells, elec_v, temp_v, adj_v, adj_grad_v, dense) = refs[10:18]
    sems = refs[18]
    held = near_far.shape[2]
    groups = held // 4
    scratch = refs[19:]
    sets = [scratch[4 * i : 4 * i + 4] for i in range(groups)]
    copies = []
    for q in range(groups):
        rows = pl.ds(16 * q, 16)
        copies.append(
            [
                pltpu.make_async_copy(far.at[:, :, rows, :], here.at[:, :, rows, :], sems.at[q, i])
                for i, (far, here) in enumerate(
                    ((elec, elec_v), (temp, temp_v), (adj_grad, adj_grad_v))
                )
            ]
            + [pltpu.make_async_copy(adj.at[:, rows, :], adj_v.at[:, rows, :], sems.at[q, 3])]
        )
        for copy in copies[q]:
            copy.start()
    outs = []

    def field_terms_at(first, count):
        rows = slice(first, first + count)
        return lambda res_x, lanes: field_pair(
            elec_v, temp_v, adj_v, adj_grad_v, scale, res_x, rows, lanes
        )

    def load_cells():
        for plane in range(2):
            flat[plane] = near_far[plane].astype(jnp.float32).reshape(flat.shape[1:])
            yield
        for b in range(held):
            for plane in range(2):
                tile = coarse_tile(flat[plane, pl.ds(b, 32, held), :])
                cells[plane, b] = tile
                if b >= held - 2:
                    last_cells[plane, b - held + 2] = tile
            if b % 2 == 1:
                yield

    def zero_sums():
        sum_three[...] = jnp.zeros_like(sum_three)
        sum_four[...] = jnp.zeros_like(sum_four)
        yield

    matrices = (m_three, m_four, m_back)
    sums = (sum_three, sum_four)
    parts = []
    for q in range(groups):
        pairs = 2 if q < groups - 1 else 1
        parts.append(Group(pairs, 4 * q, matrices, (cells,) + tuple(sets[q]), False))

    def second(q):
        for copy in copies[q]:
            copy.wait()
        count = 8 * parts[q].pairs
        rows = slice(16 * q, 16 * q + count)
        yield from parts[q].backward(
            field_terms_at(16 * q, count), dense.at[:, rows, :], sums, sums
        )
        out = pltpu.make_async_copy(
            dense.at[:, pl.ds(16 * q, count), :],
            density.at[:, pl.ds(16 * q, count), :],
            sems.at[q, 4],
        )
        out.start()
        outs.append(out)

    def last_fields():
        terms = field_terms_at(16 * groups - 8, 8)
        for res_x in range(4):
            for res_z in range(4):
                lanes = block_lanes(res_z)
                gain, loss = terms(res_x, lanes)
                last_gain[res_x, :, lanes] = gain
                last_loss[res_x, :, lanes] = loss
            yield

    fill_three(w_three, m_three, build)
    run(fill_onehot(onehot), load_cells(), zero_sums())
    fill_four(w_four, onehot, m_four, m_back)
    run(parts[0].forward())
    for q in range(groups - 1):
        run(second(q), parts[q + 1].forward())
    run(second(groups - 1), last_fields())
    for out in outs:
        out.wait()


def rim_kernel(place, rim, m_three, m_four, m_back, sum_three_in, sum_four_in, *refs):
    (onehot, last_gain, last_loss, last_cells, _) = refs[:5]
    (density, mine, other) = refs[5:8]
    (packed, sum_three, sum_four, cells, dense, sem) = refs[8:14]
    scratch = refs[14:]
    fine_rows = density.shape[1]
    for plane in range(2):
        for b in range(2):
            cells[plane, b] = last_cells[plane, b]
        cells[plane, 2] = coarse_tile(rim[plane].astype(jnp.float32))
    part = Group(1, 0, (m_three, m_four, m_back), (cells,) + tuple(scratch), True)
    run(part.forward())
    run(
        part.backward(
            lambda res_x, lanes: (last_gain[res_x, :, lanes], last_loss[res_x, :, lanes]),
            dense,
            (sum_three_in, sum_four_in),
            (sum_three, sum_four),
        )
    )
    out = pltpu.make_async_copy(dense, density.at[:, pl.ds(fine_rows - 8, 8), :], sem)
    out.start()
    by_tap = (
        sum_three[64:128, 128:],
        sum_three[:64, :128] + sum_three[128:, 128:],
        sum_three[64:128, :128],
    )
    for tap_x in range(3):
        part = by_tap[tap_x]
        packed[32 * tap_x : 32 * tap_x + 16, :] = part[48:64]
        lanes = lane_index((16, LANES))
        mixed = jnp.where(
            lanes < 64,
            part[16:32],
            jnp.where(lanes < 96, part[32:48], pltpu.roll(part[32:48], 96, 1)),
        )
        packed[32 * tap_x + 16 : 32 * tap_x + 32, :] = mixed
        packed[96:112, 32 * tap_x : 32 * tap_x + 32] = part[:16, :32]
    rest = jnp.concatenate(
        [sum_four[16 * block : 16 * block + 16, :] for block in range(BLOCKS)], 1
    )
    pieces = []
    for _ in range(3):
        piece = rest.astype(jnp.bfloat16)
        pieces.append(piece)
        rest = rest - piece.astype(jnp.float32)
    folded = matmul_nt(jnp.concatenate(pieces, 0), onehot[...])
    packed[96:112, 96:128] = folded[:16] + folded[16:32] + folded[32:48]
    which = place[0]
    half = mine.shape[0]
    mine[...] = packed[pl.ds(pl.multiple_of(which * half, 8), half), :]
    other[...] = packed[pl.ds(pl.multiple_of((1 - which) * half, 8), half), :]
    out.wait()


def unpack_kernel(part, mine, other, grad_three, grad_four):
    low = part[0] == 0
    whole = jnp.concatenate(
        [
            jnp.where(low, mine[...], other[...]),
            jnp.where(low, other[...], mine[...]),
        ],
        0,
    )
    for tap in range(27):
        row, lane = slot_of(tap)
        grad_three[tap] = whole[row : row + 16, lane : lane + 32]
    grad_four[...] = whole[96:112, 96:123]


def exchanged(value, bit_x, bit_y):
    size_x, size_y = (lax.axis_size("gx"), lax.axis_size("gy"))
    pairs = [
        (i * size_y + j, (i ^ bit_x) * size_y + (j ^ bit_y))
        for i in range(size_x)
        for j in range(size_y)
    ]
    return lax.ppermute(value, ("gx", "gy"), pairs)


def parity_of(index):
    total = index
    for shift in (1, 2, 3, 4, 5, 6, 7):
        total = total ^ (index >> shift)
    return total & 1


def sum_everywhere(mine, other, part):
    size_x, size_y = (lax.axis_size("gx"), lax.axis_size("gy"))
    assert size_x & (size_x - 1) == 0 and size_y & (size_y - 1) == 0
    assert 2 <= size_x <= 256 and size_y <= 256
    mine = mine + exchanged(other, 1, 0)
    bit = 2
    while bit < size_x:
        mine = mine + exchanged(mine, bit + 1, 0)
        bit = bit * 2
    bit = 1
    while bit < size_y:
        mine = mine + exchanged(mine, 1, bit)
        bit = bit * 2
    other = exchanged(mine, 1, 0)
    spec = pl.BlockSpec(memory_space=pltpu.VMEM)
    grad_three, grad_four = pl.pallas_call(
        unpack_kernel,
        out_shape=(
            jax.ShapeDtypeStruct((27, 16, 32), jnp.float32),
            jax.ShapeDtypeStruct((16, 27), jnp.float32),
        ),
        in_specs=[pl.BlockSpec(memory_space=pltpu.SMEM), spec, spec],
        out_specs=(spec, spec),
        compiler_params=pltpu.CompilerParams(vmem_limit_bytes=2 * MIB),
        name="unpack",
    )(part, mine, other)
    return (grad_three, grad_four.T)


def shards(coarse, w_three, w_four, elec_field, temp_grad, adjoint, adjoint_grad):
    groups_x, groups_y = (lax.axis_size("gx"), lax.axis_size("gy"))
    chan_in, count_a, held, depth = coarse.shape
    fine_x, fine_y, fine_z = adjoint.shape
    assert (fine_x, fine_y, fine_z) == (4, 4 * held, 4 * LANES)
    assert depth == LANES and chan_in == 32 and held % 4 == 0 and count_a == groups_x
    cells = fine_x * groups_x * fine_y * groups_y * fine_z
    scale = 8.0 / math.sqrt(cells)
    at_x = lax.axis_index("gx").astype(jnp.int32)
    inside = at_x + 1 < count_a
    near = lax.dynamic_index_in_dim(coarse, at_x, 1, keepdims=False)
    far = lax.dynamic_index_in_dim(coarse, jnp.minimum(at_x + 1, count_a - 1), 1, keepdims=False)
    near_far = jnp.stack([near, jnp.where(inside, far, jnp.zeros_like(far))])
    rim = lax.ppermute(near_far[:, :, 0, :], "gy", [(i + 1, i) for i in range(groups_y - 1)])
    part = parity_of(lax.axis_index("gx")) ^ parity_of(lax.axis_index("gy"))
    part = part.astype(jnp.int32).reshape(1)
    groups = held // 4

    def shape(dims, dtype):
        return jax.ShapeDtypeStruct(dims, dtype)

    def in_hbm(value):
        return pltpu.with_memory_space_constraint(value, pltpu.HBM)

    def group_scratch(pairs):
        return (
            pltpu.VMEM((WINDOW, pairs * LANES), jnp.bfloat16),
            pltpu.VMEM((192, (2 * pairs + 1) * LANES), jnp.float32),
            pltpu.VMEM((LANES, pairs * LANES), jnp.float32),
            pltpu.VMEM((192, (2 * pairs + 1) * LANES), jnp.bfloat16),
        )

    in_vmem = pl.BlockSpec(memory_space=pltpu.VMEM)
    anywhere = pl.BlockSpec(memory_space=pl.ANY)
    hbm = pl.BlockSpec(memory_space=pltpu.HBM)
    in_smem = pl.BlockSpec(memory_space=pltpu.SMEM)
    dense = shape(adjoint.shape, jnp.float32)
    handed = (
        shape((192, 256), jnp.float32),
        shape((WINDOW, LANES), jnp.float32),
        shape((192, 256), jnp.bfloat16),
        shape((LANES, WINDOW), jnp.bfloat16),
        shape((WINDOW, LANES), jnp.bfloat16),
        shape((32, BLOCKS * LANES), jnp.bfloat16),
        shape((4, 8, fine_z), jnp.float32),
        shape((4, 8, fine_z), jnp.float32),
        shape((2, 2, 64, LANES), jnp.bfloat16),
    )
    half = shape((56, LANES), jnp.float32)
    per_group = ()
    for q in range(groups):
        per_group = per_group + group_scratch(2 if q < groups - 1 else 1)
    density, sum_three, sum_four, m_three, m_four, m_back, *rest = pl.pallas_call(
        lambda *refs: interior_kernel(scale, *refs),
        out_shape=(dense,) + handed,
        in_specs=[in_vmem] * 3 + [hbm] * 4,
        out_specs=(anywhere,) + (in_vmem,) * len(handed),
        scratch_shapes=(
            pltpu.VMEM((192, 256), jnp.float32),
            pltpu.VMEM((2, chan_in * held, LANES), jnp.float32),
            pltpu.VMEM((2, held, 64, LANES), jnp.bfloat16),
            pltpu.VMEM(elec_field.shape, jnp.bfloat16),
            pltpu.VMEM(temp_grad.shape, jnp.bfloat16),
            pltpu.VMEM(adjoint.shape, jnp.bfloat16),
            pltpu.VMEM(adjoint_grad.shape, jnp.bfloat16),
            pltpu.VMEM(adjoint.shape, jnp.float32),
            pltpu.SemaphoreType.DMA((groups, 5)),
        )
        + per_group,
        compiler_params=pltpu.CompilerParams(vmem_limit_bytes=32 * MIB),
        cost_estimate=pl.CostEstimate(
            flops=2000000000, bytes_accessed=4000000, transcendentals=2000000
        ),
        name="interior",
    )(
        near_far,
        w_three,
        w_four.T,
        in_hbm(elec_field),
        in_hbm(temp_grad),
        in_hbm(adjoint),
        in_hbm(adjoint_grad),
    )
    density, mine, other = pl.pallas_call(
        rim_kernel,
        out_shape=(dense, half, half),
        in_specs=[in_smem] + [in_vmem] * (1 + len(handed)) + [anywhere],
        out_specs=(anywhere, in_vmem, in_vmem),
        scratch_shapes=(
            pltpu.VMEM((112, LANES), jnp.float32),
            pltpu.VMEM((192, 256), jnp.float32),
            pltpu.VMEM((WINDOW, LANES), jnp.float32),
            pltpu.VMEM((2, 3, 64, LANES), jnp.bfloat16),
            pltpu.VMEM((4, 8, fine_z), jnp.float32),
            pltpu.SemaphoreType.DMA(()),
        )
        + group_scratch(1),
        input_output_aliases={2 + len(handed): 0},
        compiler_params=pltpu.CompilerParams(vmem_limit_bytes=16 * MIB),
        cost_estimate=pl.CostEstimate(
            flops=400000000, bytes_accessed=2000000, transcendentals=400000
        ),
        name="rim",
    )(part, rim, m_three, m_four, m_back, sum_three, sum_four, *rest, density)
    grad_three, grad_four = sum_everywhere(mine, other, part)
    return (density, grad_three, grad_four)


def solution(mesh):
    return jax.shard_map(
        shards,
        mesh=mesh,
        in_specs=(
            P(None, None, "gy", None),
            P(),
            P(),
            P(None, "gx", "gy", None),
            P(None, "gx", "gy", None),
            P("gx", "gy", None),
            P(None, "gx", "gy", None),
        ),
        out_specs=(P("gx", "gy", None), P(), P()),
        check_vma=False,
    )
```

```python
import math

import jax
import jax.numpy as jnp
from jax import lax
from jax.experimental import pallas as pl
from jax.experimental.pallas import tpu as pltpu
from jax.sharding import PartitionSpec as P

PAIR_ROWS = 5
BLOCKS = 3 * PAIR_ROWS * 3
WINDOW = BLOCKS * 16
LANES = 128
STAGGER = 9
MIB = 1024 * 1024


def slot_of(tap):
    tap_x, tap_y, tap_z = (tap // 9, tap // 3 % 3, tap % 3)
    off_y, off_z = (int(tap_y == 0), int(tap_z == 0))
    if tap_y == 1 and tap_z == 1:
        return (96, 32 * tap_x)
    if tap_y == 1:
        return (32 * tap_x + 16, 32 * off_z)
    if tap_z == 1:
        return (32 * tap_x + 16, 64 if off_y == 1 else 96)
    return (32 * tap_x, 64 * off_y + 32 * off_z)


def lane_index(shape):
    return lax.broadcasted_iota(jnp.int32, shape, 1)


def next_lane(tile):
    moved = pltpu.roll(tile, LANES - 1, 1)
    return jnp.where(lane_index(tile.shape) == LANES - 1, 0.0, moved)


def previous_lane(tile):
    moved = pltpu.roll(tile, 1, 1)
    return jnp.where(lane_index(tile.shape) == 0, 0.0, moved)


def logistic(values):
    return 1.0 / (1.0 + jnp.exp2(values * (-1.0 / math.log(2.0))))


def matmul(left, right):
    return jnp.dot(left, right, preferred_element_type=jnp.float32)


def matmul_nt(left, right):
    return lax.dot_general(
        left, right, (((1,), (1,)), ((), ())), preferred_element_type=jnp.float32
    )


def block_lanes(block):
    return slice(block * LANES, (block + 1) * LANES)


def fill_onehot(onehot):
    tap = lax.broadcasted_iota(jnp.int32, (32, LANES), 0)
    at = lane_index((32, LANES))
    tap_x = jnp.where(tap >= 9, 1, 0) + jnp.where(tap >= 18, 1, 0)
    within = tap - 9 * tap_x
    tap_y = jnp.where(within >= 3, 1, 0) + jnp.where(within >= 6, 1, 0)
    tap_z = within - 3 * tap_y
    twice_x = (at >> 5) + 1 - tap_x
    twice_z = ((at >> 3) & 3) + 1 - tap_z
    twice_y = (at & 7) + 1 - tap_y
    code = (twice_x + 2) * 256 + (twice_y + 2) * 16 + (twice_z + 2)
    code = jnp.where(tap < 27, code, -1)
    for block in range(BLOCKS):
        src_x, src_y, src_z = (block // 15, block // 3 % 5, block % 3)
        wanted = (2 * src_x + 2) * 256 + (2 * src_y + 2) * 16 + (2 * src_z + 2)
        onehot[:, block_lanes(block)] = jnp.where(code == wanted, 1.0, 0.0).astype(jnp.bfloat16)
        if block % 5 == 4:
            yield


def fill_three(w_three, m_three, build):
    build[...] = jnp.zeros_like(build)
    for tap in range(27):
        tap_x, tap_y, tap_z = (tap // 9, tap // 3 % 3, tap % 3)
        par_y, off_y = (int(tap_y != 1), int(tap_y == 0))
        par_z, off_z = (int(tap_z != 1), int(tap_z == 0))
        row = par_y * 32 + par_z * 16
        lane = off_y * 64 + off_z * 32
        places = (((1, 1),), ((0, 0), (2, 1)), ((1, 0),))[tap_x]
        values = w_three[tap].astype(jnp.float32)
        for plane, off_x in places:
            build[
                plane * 64 + row : plane * 64 + row + 16,
                off_x * 128 + lane : off_x * 128 + lane + 32,
            ] = values
    m_three[...] = build[...].astype(jnp.bfloat16)


def fill_four(w_four, onehot, m_four, m_back):
    spread = matmul(w_four[...], onehot[:27, :])
    columns = jnp.concatenate([spread[:, block_lanes(block)] for block in range(BLOCKS)], 0)
    m_back[...] = columns.astype(jnp.bfloat16)
    m_four[...] = columns.T.astype(jnp.bfloat16)


def coarse_tile(rows):
    return jnp.concatenate([rows, next_lane(rows)], 0).astype(jnp.bfloat16)


def window_of(cells, b, last):
    after = b if last else b + 1
    return jnp.concatenate([cells[0, b], cells[0, after], cells[1, b], cells[1, after]], 0)


def field_pair(elec, temp, adj, adj_grad, scale, res_x, rows, lanes):
    energy = 0.0
    thermal = 0.0
    for comp in range(3):
        field = elec[comp, res_x, rows, lanes].astype(jnp.float32)
        energy = energy + field * field
        thermal = thermal + temp[comp, res_x, rows, lanes].astype(jnp.float32) * adj_grad[
            comp, res_x, rows, lanes
        ].astype(jnp.float32)
    gain = (scale * 3.0 * (1.0 - 0.001)) * (energy * adj[res_x, rows, lanes].astype(jnp.float32))
    return (gain, (scale * 2.0 * (1.0 - 0.01)) * thermal)


class Group:
    def __init__(self, pairs, first, matrices, scratch, top):
        self.pairs, self.first, self.top = (pairs, first, top)
        self.m_three, self.m_four, self.m_back = matrices
        self.cells, self.windows, self.slope, self.g_fine, self.g_pre = scratch
        self.hidden_rows = 4 * pairs + 1

    def window(self, b):
        return window_of(self.cells, self.first + b, self.top and b == 2 * self.pairs)

    def forward(self):
        coarse_rows = 2 * self.pairs + 1
        self.g_pre_blank()
        for b in range(coarse_rows):
            halo = b == coarse_rows - 1
            if halo:
                matrix = jnp.concatenate(
                    [self.m_three[plane * 64 : plane * 64 + 32, :] for plane in range(3)], 0
                )
                part = matmul(matrix, self.window(b))
            elif b % 2 == 0:
                both = matmul(
                    self.m_three[...],
                    jnp.concatenate([self.window(b), self.window(b + 1)], 1),
                )
                part = both[:, :LANES]
            else:
                part = both[:, LANES:]
            per_plane = 32 if halo else 64
            for plane in range(3):
                pre = part[plane * per_plane : (plane + 1) * per_plane]
                sigma = logistic(pre)
                hidden = pre * sigma
                self.slope[plane * 64 : plane * 64 + per_plane, block_lanes(b)] = (
                    sigma + hidden * (1.0 - sigma)
                )
                for par in range(per_plane // 32):
                    row = 2 * b + par
                    two = hidden[par * 32 : par * 32 + 32]
                    tall = jnp.concatenate([two, next_lane(two[:16])], 0).astype(jnp.bfloat16)
                    for pair in range(self.pairs):
                        within = row - 4 * pair
                        if 0 <= within < PAIR_ROWS:
                            start = (plane * PAIR_ROWS + within) * 48
                            self.windows[start : start + 48, block_lanes(pair)] = tall
                yield

    def g_pre_blank(self):
        for plane in range(3):
            self.g_pre[plane * 64 + 32 : plane * 64 + 64, block_lanes(2 * self.pairs)] = jnp.zeros(
                (32, LANES), jnp.bfloat16
            )

    def middle(self, field_terms, density):
        logits = matmul(self.m_four[...], self.windows[...])
        yield
        for res_x in range(4):
            for res_z in range(4):
                at = (res_x * 4 + res_z) * 8
                lanes = block_lanes(res_z)
                d = logistic(
                    jnp.concatenate(
                        [logits[at : at + 8, block_lanes(pair)] for pair in range(self.pairs)], 0
                    )
                )
                density[res_x, :, lanes] = d
                gain, loss = field_terms(res_x, lanes)
                g = d * d * (1.0 - d) * (gain * d - loss)
                for pair in range(self.pairs):
                    self.g_fine[at : at + 8, block_lanes(pair)] = g[8 * pair : 8 * pair + 8]
                if res_z % 2 == 1:
                    yield

    def backward(self, sums_from, sums_to):
        g_out = self.g_fine[...].astype(jnp.bfloat16)
        for plane in range(3):
            span = slice(plane * 240, plane * 240 + 240)
            spread = matmul(self.m_back[span, :], g_out)
            for row in range(self.hidden_rows):
                tall = 0.0
                for pair in range(self.pairs):
                    within = row - 4 * pair
                    if 0 <= within < PAIR_ROWS:
                        tall = tall + spread[within * 48 : within * 48 + 48, block_lanes(pair)]
                both = jnp.concatenate([tall[:16] + previous_lane(tall[32:]), tall[16:32]], 0)
                at = plane * 64 + row % 2 * 32
                lanes = block_lanes(row // 2)
                if plane == 1 and 0 < row < self.hidden_rows - 1:
                    both = both.astype(jnp.bfloat16).astype(jnp.float32)
                self.g_pre[at : at + 32, lanes] = (
                    both * self.slope[at : at + 32, lanes]
                ).astype(jnp.bfloat16)
            yield
            sums_to[1][span, :] = sums_from[1][span, :] + matmul_nt(self.windows[span, :], g_out)
            yield
        wide = jnp.concatenate([self.window(b) for b in range(2 * self.pairs + 1)], 1)
        sums_to[0][...] = sums_from[0][...] + matmul_nt(self.g_pre[...], wide)
        yield


def run(*streams):
    live = list(streams)
    while live:
        for entry in list(live):
            stream, count = entry
            for _ in range(count):
                if next(stream, live) is live:
                    live.remove(entry)
                    break


def staggered(pending, side, apart):
    live = []
    turn = 0
    while pending or live or side:
        if pending and turn % apart == 0:
            live.append(pending.pop(0))
        for stream in live + side[:1]:
            if next(stream, live) is live:
                (live if stream in live else side).remove(stream)
        turn = turn + 1


def chain(*streams):
    for stream in streams:
        yield from stream


def interior_kernel(scale, inside, near, far, *refs):
    (w_three_far, w_four_far, elec, temp, adj, adj_grad) = refs[:6]
    refs = refs[6:]
    (dense, sum_three, sum_four, m_three, m_four, m_back) = refs[:6]
    (onehot, last_gain, last_loss, last_cells) = refs[6:10]
    (build, flat, cells, elec_v, temp_v, adj_v, adj_grad_v) = refs[10:17]
    (w_three, w_four, sems) = refs[17:20]
    held = near.shape[1]
    groups = held // 4
    scratch = refs[20:]
    weights = (
        pltpu.make_async_copy(w_three_far, w_three, sems.at[0, 5]),
        pltpu.make_async_copy(w_four_far, w_four, sems.at[1, 5]),
    )
    for copy in weights:
        copy.start()
    sets = [scratch[4 * i : 4 * i + 4] for i in range(groups)]
    copies = []
    for q in range(groups):
        rows = pl.ds(16 * q, 16)
        copies.append(
            [
                pltpu.make_async_copy(far.at[:, :, rows, :], here.at[:, :, rows, :], sems.at[q, i])
                for i, (far, here) in enumerate(
                    ((elec, elec_v), (temp, temp_v), (adj_grad, adj_grad_v))
                )
            ]
            + [pltpu.make_async_copy(adj.at[:, rows, :], adj_v.at[:, rows, :], sems.at[q, 3])]
        )
        for copy in copies[q]:
            copy.start()

    def field_terms_at(first, count):
        rows = slice(first, first + count)
        return lambda res_x, lanes: field_pair(
            elec_v, temp_v, adj_v, adj_grad_v, scale, res_x, rows, lanes
        )

    def flatten():
        flat[0] = near[...].astype(jnp.float32).reshape(flat.shape[1:])
        yield
        known = inside[0].astype(jnp.float32)
        flat[1] = known * far[...].astype(jnp.float32).reshape(flat.shape[1:])
        yield

    def load_cells(first, end):
        for b in range(first, end):
            for plane in range(2):
                tile = coarse_tile(flat[plane, pl.ds(b, 32, held), :])
                cells[plane, b] = tile
                if b >= held - 2:
                    last_cells[plane, b - held + 2] = tile
            yield

    def zero_sums():
        sum_three[...] = jnp.zeros_like(sum_three)
        yield
        sum_four[...] = jnp.zeros_like(sum_four)
        yield

    matrices = (m_three, m_four, m_back)
    sums = (sum_three, sum_four)
    parts = []
    for q in range(groups):
        pairs = 2 if q < groups - 1 else 1
        parts.append(Group(pairs, 4 * q, matrices, (cells,) + tuple(sets[q]), False))

    def middle(q):
        count = 8 * parts[q].pairs
        rows = slice(16 * q, 16 * q + count)
        yield from parts[q].middle(field_terms_at(16 * q, count), dense.at[:, rows, :])

    def last_fields():
        terms = field_terms_at(16 * groups - 8, 8)
        for res_x in range(4):
            for res_z in range(4):
                lanes = block_lanes(res_z)
                gain, loss = terms(res_x, lanes)
                last_gain[res_x, :, lanes] = gain
                last_loss[res_x, :, lanes] = loss
            yield

    def fill_late():
        yield from fill_onehot(onehot)
        weights[1].wait()
        fill_four(w_four, onehot, m_four, m_back)
        yield

    run((flatten(), 1))
    run((load_cells(0, 5), 1))
    weights[0].wait()
    fill_three(w_three, m_three, build)
    run((parts[0].forward(), 2), (fill_late(), 1), (load_cells(5, 9), 1), (zero_sums(), 1))
    for group_copies in copies:
        for copy in group_copies:
            copy.wait()
    later = [load_cells(9, held), last_fields()]
    pending = [
        chain(parts[q].forward() if q > 0 else (), middle(q), parts[q].backward(sums, sums))
        for q in range(groups)
    ]
    staggered(pending, later, STAGGER)


def rim_kernel(part, inside, rim, sum_three_in, sum_four_in, *refs):
    (m_three, m_four, m_back, onehot, last_gain, last_loss, last_cells) = refs[:7]
    (dense, mine, other) = refs[7:10]
    (packed, sum_three, sum_four, cells) = refs[10:14]
    scratch = refs[14:]
    known = (1.0, inside[0].astype(jnp.float32))
    for plane in range(2):
        for b in range(2):
            cells[plane, b] = last_cells[plane, b]
        cells[plane, 2] = coarse_tile(known[plane] * rim[plane].astype(jnp.float32))
    group = Group(1, 0, (m_three, m_four, m_back), (cells,) + tuple(scratch), True)
    run((group.forward(), 1))
    terms = lambda res_x, lanes: (last_gain[res_x, :, lanes], last_loss[res_x, :, lanes])
    run((group.middle(terms, dense), 1))
    run((group.backward((sum_three_in, sum_four_in), (sum_three, sum_four)), 1))
    by_tap = (
        sum_three[64:128, 128:],
        sum_three[:64, :128] + sum_three[128:, 128:],
        sum_three[64:128, :128],
    )
    for tap_x in range(3):
        along = by_tap[tap_x]
        packed[32 * tap_x : 32 * tap_x + 16, :] = along[48:64]
        lanes = lane_index((16, LANES))
        mixed = jnp.where(
            lanes < 64,
            along[16:32],
            jnp.where(lanes < 96, along[32:48], pltpu.roll(along[32:48], 96, 1)),
        )
        packed[32 * tap_x + 16 : 32 * tap_x + 32, :] = mixed
        packed[96:112, 32 * tap_x : 32 * tap_x + 32] = along[:16, :32]
    rest = jnp.concatenate(
        [sum_four[16 * block : 16 * block + 16, :] for block in range(BLOCKS)], 1
    )
    pieces = []
    for _ in range(3):
        piece = rest.astype(jnp.bfloat16)
        pieces.append(piece)
        rest = rest - piece.astype(jnp.float32)
    folded = matmul_nt(jnp.concatenate(pieces, 0), onehot[...])
    packed[96:112, 96:128] = folded[:16] + folded[16:32] + folded[32:48]
    which = part[0]
    half = mine.shape[0]
    mine[...] = packed[pl.ds(pl.multiple_of(which * half, 8), half), :]
    other[...] = packed[pl.ds(pl.multiple_of((1 - which) * half, 8), half), :]


def unpack_kernel(part, mine, other, grad_three, grad_four):
    low = part[0] == 0
    whole = jnp.concatenate(
        [
            jnp.where(low, mine[...], other[...]),
            jnp.where(low, other[...], mine[...]),
        ],
        0,
    )
    for tap in range(27):
        row, lane = slot_of(tap)
        grad_three[tap] = whole[row : row + 16, lane : lane + 32]
    grad_four[...] = whole[96:112, 96:123]


def exchanged(value, bit_x, bit_y):
    size_x, size_y = (lax.axis_size("gx"), lax.axis_size("gy"))
    pairs = [
        (i * size_y + j, (i ^ bit_x) * size_y + (j ^ bit_y))
        for i in range(size_x)
        for j in range(size_y)
    ]
    return lax.ppermute(value, ("gx", "gy"), pairs)


def parity_of(index):
    total = index
    for shift in (1, 2, 3, 4, 5, 6, 7):
        total = total ^ (index >> shift)
    return total & 1


def sum_everywhere(mine, other, part):
    size_x, size_y = (lax.axis_size("gx"), lax.axis_size("gy"))
    assert size_x & (size_x - 1) == 0 and size_y & (size_y - 1) == 0
    assert 2 <= size_x <= 256 and size_y <= 256
    mine = mine + exchanged(other, 1, 0)
    bit = 2
    while bit < size_x:
        mine = mine + exchanged(mine, bit + 1, 0)
        bit = bit * 2
    bit = 1
    while bit < size_y:
        mine = mine + exchanged(mine, 1, bit)
        bit = bit * 2
    other = exchanged(mine, 1, 0)
    spec = pl.BlockSpec(memory_space=pltpu.VMEM)
    grad_three, grad_four = pl.pallas_call(
        unpack_kernel,
        out_shape=(
            jax.ShapeDtypeStruct((27, 16, 32), jnp.float32),
            jax.ShapeDtypeStruct((16, 27), jnp.float32),
        ),
        in_specs=[pl.BlockSpec(memory_space=pltpu.SMEM), spec, spec],
        out_specs=(spec, spec),
        compiler_params=pltpu.CompilerParams(vmem_limit_bytes=2 * MIB),
        name="unpack",
    )(part, mine, other)
    return (grad_three, grad_four.T)


def shards(coarse, w_three, w_four, elec_field, temp_grad, adjoint, adjoint_grad):
    groups_x, groups_y = (lax.axis_size("gx"), lax.axis_size("gy"))
    chan_in, count_a, held, depth = coarse.shape
    fine_x, fine_y, fine_z = adjoint.shape
    assert (fine_x, fine_y, fine_z) == (4, 4 * held, 4 * LANES)
    assert depth == LANES and chan_in == 32 and held % 4 == 0 and count_a == groups_x
    cells = fine_x * groups_x * fine_y * groups_y * fine_z
    scale = 8.0 / math.sqrt(cells)
    at_x = lax.axis_index("gx").astype(jnp.int32)
    inside = at_x + 1 < count_a
    near = lax.dynamic_index_in_dim(coarse, at_x, 1, keepdims=False)
    far = lax.dynamic_index_in_dim(coarse, jnp.minimum(at_x + 1, count_a - 1), 1, keepdims=False)
    first_rows = jnp.stack([near[:, 0], far[:, 0]])
    rim = lax.ppermute(first_rows, "gy", [(i + 1, i) for i in range(groups_y - 1)])
    inside = inside.astype(jnp.int32).reshape(1)
    part = parity_of(lax.axis_index("gx")) ^ parity_of(lax.axis_index("gy"))
    part = part.astype(jnp.int32).reshape(1)
    groups = held // 4

    def shape(dims, dtype):
        return jax.ShapeDtypeStruct(dims, dtype)

    def in_hbm(value):
        return pltpu.with_memory_space_constraint(value, pltpu.HBM)

    def group_scratch(pairs):
        return (
            pltpu.VMEM((WINDOW, pairs * LANES), jnp.bfloat16),
            pltpu.VMEM((192, (2 * pairs + 1) * LANES), jnp.float32),
            pltpu.VMEM((LANES, pairs * LANES), jnp.float32),
            pltpu.VMEM((192, (2 * pairs + 1) * LANES), jnp.bfloat16),
        )

    in_vmem = pl.BlockSpec(memory_space=pltpu.VMEM)
    hbm = pl.BlockSpec(memory_space=pltpu.HBM)
    in_smem = pl.BlockSpec(memory_space=pltpu.SMEM)
    handed = (
        shape((fine_x, fine_y - 8, fine_z), jnp.float32),
        shape((192, 256), jnp.float32),
        shape((WINDOW, LANES), jnp.float32),
        shape((192, 256), jnp.bfloat16),
        shape((LANES, WINDOW), jnp.bfloat16),
        shape((WINDOW, LANES), jnp.bfloat16),
        shape((32, BLOCKS * LANES), jnp.bfloat16),
        shape((4, 8, fine_z), jnp.float32),
        shape((4, 8, fine_z), jnp.float32),
        shape((2, 2, 64, LANES), jnp.bfloat16),
    )
    half = shape((56, LANES), jnp.float32)
    per_group = ()
    for q in range(groups):
        per_group = per_group + group_scratch(2 if q < groups - 1 else 1)
    most, *held_back = pl.pallas_call(
        lambda *refs: interior_kernel(scale, *refs),
        out_shape=handed,
        in_specs=[in_smem] + [in_vmem] * 2 + [hbm] * 6,
        out_specs=(in_vmem,) * len(handed),
        scratch_shapes=(
            pltpu.VMEM((192, 256), jnp.float32),
            pltpu.VMEM((2, chan_in * held, LANES), jnp.float32),
            pltpu.VMEM((2, held, 64, LANES), jnp.bfloat16),
            pltpu.VMEM(elec_field.shape, jnp.bfloat16),
            pltpu.VMEM(temp_grad.shape, jnp.bfloat16),
            pltpu.VMEM(adjoint.shape, jnp.bfloat16),
            pltpu.VMEM(adjoint_grad.shape, jnp.bfloat16),
            pltpu.VMEM(w_three.shape, jnp.bfloat16),
            pltpu.VMEM(w_four.shape[::-1], jnp.bfloat16),
            pltpu.SemaphoreType.DMA((groups, 6)),
        )
        + per_group,
        compiler_params=pltpu.CompilerParams(vmem_limit_bytes=32 * MIB),
        cost_estimate=pl.CostEstimate(
            flops=2000000000, bytes_accessed=4000000, transcendentals=2000000
        ),
        name="interior",
    )(
        inside,
        near,
        far,
        in_hbm(w_three),
        in_hbm(w_four.T),
        in_hbm(elec_field),
        in_hbm(temp_grad),
        in_hbm(adjoint),
        in_hbm(adjoint_grad),
    )
    last_dense, mine, other = pl.pallas_call(
        rim_kernel,
        out_shape=(shape((fine_x, 8, fine_z), jnp.float32), half, half),
        in_specs=[in_smem] * 2 + [in_vmem] * len(handed),
        out_specs=(in_vmem,) * 3,
        scratch_shapes=(
            pltpu.VMEM((112, LANES), jnp.float32),
            pltpu.VMEM((192, 256), jnp.float32),
            pltpu.VMEM((WINDOW, LANES), jnp.float32),
            pltpu.VMEM((2, 3, 64, LANES), jnp.bfloat16),
        )
        + group_scratch(1),
        compiler_params=pltpu.CompilerParams(vmem_limit_bytes=16 * MIB),
        cost_estimate=pl.CostEstimate(
            flops=400000000, bytes_accessed=2000000, transcendentals=400000
        ),
        name="rim",
    )(part, inside, rim, *held_back)
    density = jnp.concatenate([most, last_dense], 1)
    grad_three, grad_four = sum_everywhere(mine, other, part)
    return (density, grad_three, grad_four)


def solution(mesh):
    return jax.shard_map(
        shards,
        mesh=mesh,
        in_specs=(
            P(None, None, "gy", None),
            P(),
            P(),
            P(None, "gx", "gy", None),
            P(None, "gx", "gy", None),
            P("gx", "gy", None),
            P(None, "gx", "gy", None),
        ),
        out_specs=(P("gx", "gy", None), P(), P()),
        check_vma=False,
    )
```

```python
import math

import jax
import jax.numpy as jnp
from jax import lax
from jax.experimental import pallas as pl
from jax.experimental.pallas import tpu as pltpu
from jax.sharding import PartitionSpec as P

PAIR_ROWS = 5
BLOCKS = 3 * PAIR_ROWS * 3
WINDOW = BLOCKS * 16
LANES = 128
FRONT_APART = 5
BACK_APART = 5
MIB = 1024 * 1024


def slot_of(tap):
    tap_x, tap_y, tap_z = (tap // 9, tap // 3 % 3, tap % 3)
    off_y, off_z = (int(tap_y == 0), int(tap_z == 0))
    if tap_y == 1 and tap_z == 1:
        return (96, 32 * tap_x)
    if tap_y == 1:
        return (32 * tap_x + 16, 32 * off_z)
    if tap_z == 1:
        return (32 * tap_x + 16, 64 if off_y == 1 else 96)
    return (32 * tap_x, 64 * off_y + 32 * off_z)


def lane_index(shape):
    return lax.broadcasted_iota(jnp.int32, shape, 1)


def next_lane(tile):
    moved = pltpu.roll(tile, LANES - 1, 1)
    return jnp.where(lane_index(tile.shape) == LANES - 1, jnp.zeros_like(tile), moved)


def previous_lane(tile):
    moved = pltpu.roll(tile, 1, 1)
    return jnp.where(lane_index(tile.shape) == 0, 0.0, moved)


def logistic(values):
    return 1.0 / (1.0 + jnp.exp2(values * (-1.0 / math.log(2.0))))


def matmul(left, right):
    return jnp.dot(left, right, preferred_element_type=jnp.float32)


def matmul_nt(left, right):
    return lax.dot_general(
        left, right, (((1,), (1,)), ((), ())), preferred_element_type=jnp.float32
    )


def block_lanes(block):
    return slice(block * LANES, (block + 1) * LANES)


def fill_onehot(onehot):
    tap = lax.broadcasted_iota(jnp.int32, (32, LANES), 0)
    at = lane_index((32, LANES))
    tap_x = jnp.where(tap >= 9, 1, 0) + jnp.where(tap >= 18, 1, 0)
    within = tap - 9 * tap_x
    tap_y = jnp.where(within >= 3, 1, 0) + jnp.where(within >= 6, 1, 0)
    tap_z = within - 3 * tap_y
    twice_x = (at >> 5) + 1 - tap_x
    twice_z = ((at >> 3) & 3) + 1 - tap_z
    twice_y = (at & 7) + 1 - tap_y
    odd = (twice_x | twice_y | twice_z) & 1
    inside = jnp.minimum(jnp.minimum(twice_x, twice_y), twice_z)
    block_of = (twice_x >> 1) * 15 + (twice_y >> 1) * 3 + (twice_z >> 1)
    known = jnp.where(odd == 0, block_of, -1)
    known = jnp.where(inside >= 0, known, -1)
    known = jnp.where(tap < 27, known, -1).astype(jnp.float32).astype(jnp.bfloat16)
    one, zero = (jnp.ones((32, LANES), jnp.bfloat16), jnp.zeros((32, LANES), jnp.bfloat16))
    for block in range(BLOCKS):
        onehot[:, block_lanes(block)] = jnp.where(known == jnp.bfloat16(block), one, zero)
        if block % 5 == 4:
            yield


def fill_three(w_three, m_three, build):
    build[...] = jnp.zeros_like(build)
    for tap in range(27):
        tap_x, tap_y, tap_z = (tap // 9, tap // 3 % 3, tap % 3)
        par_y, off_y = (int(tap_y != 1), int(tap_y == 0))
        par_z, off_z = (int(tap_z != 1), int(tap_z == 0))
        row = par_y * 32 + par_z * 16
        lane = off_y * 64 + off_z * 32
        places = (((1, 1),), ((0, 0), (2, 1)), ((1, 0),))[tap_x]
        values = w_three[tap].astype(jnp.float32)
        for plane, off_x in places:
            build[
                plane * 64 + row : plane * 64 + row + 16,
                off_x * 128 + lane : off_x * 128 + lane + 32,
            ] = values
    m_three[...] = build[...].astype(jnp.bfloat16)


def fill_four(w_four, onehot, m_four, m_back):
    spread = matmul(w_four[...], onehot[:27, :])
    columns = jnp.concatenate([spread[:, block_lanes(block)] for block in range(BLOCKS)], 0)
    m_back[...] = columns.astype(jnp.bfloat16)
    m_four[...] = columns.astype(jnp.bfloat16).T


def coarse_tile(rows):
    return jnp.concatenate([rows, next_lane(rows)], 0)


def window_of(cells, b, last):
    after = b if last else b + 1
    return jnp.concatenate([cells[0, b], cells[0, after], cells[1, b], cells[1, after]], 0)


def field_pair(elec, temp, adj, adj_grad, scale, res_x, rows, lanes):
    energy = 0.0
    thermal = 0.0
    for comp in range(3):
        field = elec[comp, res_x, rows, lanes].astype(jnp.float32)
        energy = energy + field * field
        thermal = thermal + temp[comp, res_x, rows, lanes].astype(jnp.float32) * adj_grad[
            comp, res_x, rows, lanes
        ].astype(jnp.float32)
    gain = (scale * 3.0 * (1.0 - 0.001)) * (energy * adj[res_x, rows, lanes].astype(jnp.float32))
    return (gain, (scale * 2.0 * (1.0 - 0.01)) * thermal)


class Group:
    def __init__(self, pairs, first, matrices, scratch, top):
        self.pairs, self.first, self.top = (pairs, first, top)
        self.m_three, self.m_four, self.m_back = matrices
        self.cells, self.windows, self.slope, self.g_fine, self.g_pre = scratch
        self.hidden_rows = 4 * pairs + 1

    def window(self, b):
        return window_of(self.cells, self.first + b, self.top and b == 2 * self.pairs)

    def forward(self):
        coarse_rows = 2 * self.pairs + 1
        self.g_pre_blank()
        for b in range(coarse_rows):
            halo = b == coarse_rows - 1
            if halo:
                matrix = jnp.concatenate(
                    [self.m_three[plane * 64 : plane * 64 + 32, :] for plane in range(3)], 0
                )
                part = matmul(matrix, self.window(b))
            elif b % 2 == 0:
                both = matmul(
                    self.m_three[...],
                    jnp.concatenate([self.window(b), self.window(b + 1)], 1),
                )
                part = both[:, :LANES]
            else:
                part = both[:, LANES:]
            per_plane = 32 if halo else 64
            for plane in range(3):
                pre = part[plane * per_plane : (plane + 1) * per_plane]
                sigma = logistic(pre)
                hidden = pre * sigma
                self.slope[plane * 64 : plane * 64 + per_plane, block_lanes(b)] = (
                    sigma + hidden * (1.0 - sigma)
                )
                for par in range(per_plane // 32):
                    row = 2 * b + par
                    two = hidden[par * 32 : par * 32 + 32].astype(jnp.bfloat16)
                    tall = jnp.concatenate([two, next_lane(two[:16])], 0)
                    for pair in range(self.pairs):
                        within = row - 4 * pair
                        if 0 <= within < PAIR_ROWS:
                            start = (plane * PAIR_ROWS + within) * 48
                            self.windows[start : start + 48, block_lanes(pair)] = tall
                yield

    def g_pre_blank(self):
        for plane in range(3):
            self.g_pre[plane * 64 + 32 : plane * 64 + 64, block_lanes(2 * self.pairs)] = jnp.zeros(
                (32, LANES), jnp.bfloat16
            )

    def solid(self, density):
        logits = matmul(self.m_four[...], self.windows[...])
        yield
        for res_x in range(4):
            for res_z in range(4):
                at = (res_x * 4 + res_z) * 8
                density[res_x, :, block_lanes(res_z)] = logistic(
                    jnp.concatenate(
                        [logits[at : at + 8, block_lanes(pair)] for pair in range(self.pairs)], 0
                    )
                )
            yield

    def middle(self, field_terms, density):
        for res_x in range(4):
            for res_z in range(4):
                at = (res_x * 4 + res_z) * 8
                lanes = block_lanes(res_z)
                d = density[res_x, :, lanes]
                gain, loss = field_terms(res_x, lanes)
                g = d * d * (1.0 - d) * (gain * d - loss)
                if res_z % 2 == 0:
                    before = g
                    continue
                for pair in range(self.pairs):
                    rows = slice(8 * pair, 8 * pair + 8)
                    self.g_fine[at - 8 : at + 8, block_lanes(pair)] = jnp.concatenate(
                        [before[rows], g[rows]], 0
                    ).astype(jnp.bfloat16)
                yield

    def backward(self, sums_from, sums_to):
        g_out = self.g_fine[...]
        for plane in range(3):
            span = slice(plane * 240, plane * 240 + 240)
            spread = matmul(self.m_back[span, :], g_out)
            for row in range(self.hidden_rows):
                tall = 0.0
                for pair in range(self.pairs):
                    within = row - 4 * pair
                    if 0 <= within < PAIR_ROWS:
                        tall = tall + spread[within * 48 : within * 48 + 48, block_lanes(pair)]
                both = jnp.concatenate([tall[:16] + previous_lane(tall[32:]), tall[16:32]], 0)
                at = plane * 64 + row % 2 * 32
                lanes = block_lanes(row // 2)
                if plane == 1 and 0 < row < self.hidden_rows - 1:
                    both = both.astype(jnp.bfloat16).astype(jnp.float32)
                self.g_pre[at : at + 32, lanes] = (
                    both * self.slope[at : at + 32, lanes]
                ).astype(jnp.bfloat16)
            yield
            sums_to[1][span, :] = sums_from[1][span, :] + matmul_nt(self.windows[span, :], g_out)
            yield
        wide = jnp.concatenate([self.window(b) for b in range(2 * self.pairs + 1)], 1)
        sums_to[0][...] = sums_from[0][...] + matmul_nt(self.g_pre[...], wide)
        yield


def run(*streams):
    live = list(streams)
    while live:
        for entry in list(live):
            stream, count = entry
            for _ in range(count):
                if next(stream, live) is live:
                    live.remove(entry)
                    break


def staggered(pending, side, apart):
    live = []
    turn = 0
    while pending or live or side:
        if pending and turn % apart == 0:
            live.append(pending.pop(0))
        for stream in live + side[:1]:
            if next(stream, live) is live:
                (live if stream in live else side).remove(stream)
        turn = turn + 1


def chain(*streams):
    for stream in streams:
        yield from stream


def fetch_kernel(at_x, coarse, *refs):
    sems = refs[-1]
    count = (len(refs) - 4) // 2
    last = coarse.shape[1] - 1
    base = at_x[0] - lax.rem(at_x[0], 2)
    copies = [
        pltpu.make_async_copy(coarse.at[:, jnp.minimum(base + i, last), :, :], here, sems.at[i])
        for i, here in enumerate(refs[count : count + 3])
    ]
    copies = copies + [
        pltpu.make_async_copy(refs[i], refs[count + 3 + i], sems.at[3 + i]) for i in range(count)
    ]
    for copy in copies:
        copy.start()
    for copy in copies:
        copy.wait()


def interior_kernel(scale, core, inside, *refs):
    (plane_a, plane_b, plane_c, w_three, w_four, elec, adj, temp, adj_grad) = refs[:9]
    refs = refs[9:]
    (dense, sum_three, sum_four, m_three, m_four, m_back) = refs[:6]
    (onehot, last_gain, last_loss, last_cells) = refs[6:10]
    (build, cells, elec_v, adj_v, temp_v, adj_grad_v, sems) = refs[10:17]
    held = plane_a.shape[0]
    groups = held // 4
    scratch = refs[17:]
    sets = [scratch[4 * i : 4 * i + 4] for i in range(groups)]
    def copies_of(comp):
        return [
            pltpu.make_async_copy(far.at[comp], here.at[comp], sems.at[comp, i])
            for i, (far, here) in enumerate(
                ((elec, elec_v), (temp, temp_v), (adj_grad, adj_grad_v))
            )
        ]

    def start_copies(comp, carry):
        for copy in copies_of(comp):
            copy.start()
        return carry

    adjoint_copy = pltpu.make_async_copy(adj, adj_v, sems.at[0, 3])
    adjoint_copy.start()
    lax.fori_loop(0, 3, start_copies, 0)

    def field_terms_at(first, count):
        rows = slice(first, first + count)
        return lambda res_x, lanes: field_pair(
            elec_v, temp_v, adj_v, adj_grad_v, scale, res_x, rows, lanes
        )

    known = inside[0].astype(jnp.float32).astype(jnp.bfloat16)

    def load_cells():
        low = core[0] == 0
        for b in range(held):
            near = jnp.where(low, plane_a[b], plane_b[b])
            far = known * jnp.where(low, plane_b[b], plane_c[b])
            for plane, rows in enumerate((near, far)):
                tile = coarse_tile(rows)
                cells[plane, b] = tile
                if b >= held - 2:
                    last_cells[plane, b - held + 2] = tile
            yield

    def zero_sums():
        sum_three[...] = jnp.zeros_like(sum_three)
        yield
        sum_four[...] = jnp.zeros_like(sum_four)
        yield

    matrices = (m_three, m_four, m_back)
    sums = (sum_three, sum_four)
    parts = []
    for q in range(groups):
        pairs = 2 if q < groups - 1 else 1
        parts.append(Group(pairs, 4 * q, matrices, (cells,) + tuple(sets[q]), False))

    def front(q):
        yield from parts[q].forward()
        yield from parts[q].solid(dense.at[:, rows_of(q), :])

    def back(q):
        yield from parts[q].middle(
            field_terms_at(16 * q, 8 * parts[q].pairs), dense.at[:, rows_of(q), :]
        )
        yield from parts[q].backward(sums, sums)

    def rows_of(q):
        return slice(16 * q, 16 * q + 8 * parts[q].pairs)

    def last_fields():
        terms = field_terms_at(16 * groups - 8, 8)
        for res_x in range(4):
            for res_z in range(4):
                lanes = block_lanes(res_z)
                gain, loss = terms(res_x, lanes)
                last_gain[res_x, :, lanes] = gain
                last_loss[res_x, :, lanes] = loss
            yield

    run((fill_onehot(onehot), 1), (load_cells(), 2), (zero_sums(), 1))
    fill_four(w_four, onehot, m_four, m_back)
    fill_three(w_three, m_three, build)
    staggered([front(q) for q in range(groups)], [], FRONT_APART)
    adjoint_copy.wait()
    for comp in range(3):
        for copy in copies_of(comp):
            copy.wait()
    staggered([back(q) for q in range(groups)], [last_fields()], BACK_APART)


def rim_kernel(part, inside, rim, sum_three_in, sum_four_in, *refs):
    (m_three, m_four, m_back, onehot, last_gain, last_loss, last_cells) = refs[:7]
    (dense, mine, other) = refs[7:10]
    (packed, sum_three, sum_four, cells) = refs[10:14]
    scratch = refs[14:]
    known = inside[0].astype(jnp.float32).astype(jnp.bfloat16)
    for plane in range(2):
        for b in range(2):
            cells[plane, b] = last_cells[plane, b]
        cells[plane, 2] = coarse_tile(rim[plane] if plane == 0 else known * rim[plane])
    group = Group(1, 0, (m_three, m_four, m_back), (cells,) + tuple(scratch), True)
    run((group.forward(), 1))
    terms = lambda res_x, lanes: (last_gain[res_x, :, lanes], last_loss[res_x, :, lanes])
    run((group.solid(dense), 1))
    run((group.middle(terms, dense), 1))
    run((group.backward((sum_three_in, sum_four_in), (sum_three, sum_four)), 1))
    by_tap = (
        sum_three[64:128, 128:],
        sum_three[:64, :128] + sum_three[128:, 128:],
        sum_three[64:128, :128],
    )
    for tap_x in range(3):
        along = by_tap[tap_x]
        packed[32 * tap_x : 32 * tap_x + 16, :] = along[48:64]
        lanes = lane_index((16, LANES))
        mixed = jnp.where(
            lanes < 64,
            along[16:32],
            jnp.where(lanes < 96, along[32:48], pltpu.roll(along[32:48], 96, 1)),
        )
        packed[32 * tap_x + 16 : 32 * tap_x + 32, :] = mixed
        packed[96:112, 32 * tap_x : 32 * tap_x + 32] = along[:16, :32]
    rest = jnp.concatenate(
        [sum_four[16 * block : 16 * block + 16, :] for block in range(BLOCKS)], 1
    )
    pieces = []
    for _ in range(3):
        piece = rest.astype(jnp.bfloat16)
        pieces.append(piece)
        rest = rest - piece.astype(jnp.float32)
    folded = matmul_nt(jnp.concatenate(pieces, 0), onehot[...])
    packed[96:112, 96:128] = folded[:16] + folded[16:32] + folded[32:48]
    which = part[0]
    half = mine.shape[0]
    mine[...] = packed[pl.ds(pl.multiple_of(which * half, 8), half), :]
    other[...] = packed[pl.ds(pl.multiple_of((1 - which) * half, 8), half), :]


def unpack_kernel(part, mine, other, grad_three, grad_four):
    low = part[0] == 0
    whole = jnp.concatenate(
        [
            jnp.where(low, mine[...], other[...]),
            jnp.where(low, other[...], mine[...]),
        ],
        0,
    )
    for tap in range(27):
        row, lane = slot_of(tap)
        grad_three[tap] = whole[row : row + 16, lane : lane + 32]
    grad_four[...] = whole[96:112, 96:123]


def exchanged(value, bit_x, bit_y):
    size_x, size_y = (lax.axis_size("gx"), lax.axis_size("gy"))
    pairs = [
        (i * size_y + j, (i ^ bit_x) * size_y + (j ^ bit_y))
        for i in range(size_x)
        for j in range(size_y)
    ]
    return lax.ppermute(value, ("gx", "gy"), pairs)


def parity_of(index):
    total = index
    for shift in (1, 2, 3, 4, 5, 6, 7):
        total = total ^ (index >> shift)
    return total & 1


def sum_everywhere(mine, other, part):
    size_x, size_y = (lax.axis_size("gx"), lax.axis_size("gy"))
    assert size_x & (size_x - 1) == 0 and size_y & (size_y - 1) == 0
    assert 2 <= size_x <= 256 and size_y <= 256
    mine = mine + exchanged(other, 1, 0)
    bit = 2
    while bit < size_x:
        mine = mine + exchanged(mine, bit + 1, 0)
        bit = bit * 2
    bit = 1
    while bit < size_y:
        mine = mine + exchanged(mine, 1, bit)
        bit = bit * 2
    other = exchanged(mine, 1, 0)
    spec = pl.BlockSpec(memory_space=pltpu.VMEM)
    grad_three, grad_four = pl.pallas_call(
        unpack_kernel,
        out_shape=(
            jax.ShapeDtypeStruct((27, 16, 32), jnp.float32),
            jax.ShapeDtypeStruct((16, 27), jnp.float32),
        ),
        in_specs=[pl.BlockSpec(memory_space=pltpu.SMEM), spec, spec],
        out_specs=(spec, spec),
        compiler_params=pltpu.CompilerParams(vmem_limit_bytes=2 * MIB),
        name="unpack",
    )(part, mine, other)
    return (grad_three, grad_four.T)


def shards(coarse, w_three, w_four, elec_field, temp_grad, adjoint, adjoint_grad):
    groups_x, groups_y = (lax.axis_size("gx"), lax.axis_size("gy"))
    chan_in, count_a, held, depth = coarse.shape
    fine_x, fine_y, fine_z = adjoint.shape
    assert (fine_x, fine_y, fine_z) == (4, 4 * held, 4 * LANES)
    assert depth == LANES and chan_in == 32 and held % 4 == 0 and count_a == groups_x
    cells = fine_x * groups_x * fine_y * groups_y * fine_z
    scale = 8.0 / math.sqrt(cells)
    at_x = lax.axis_index("gx").astype(jnp.int32)
    inside = (at_x + 1 < count_a).astype(jnp.int32).reshape(1)
    core = at_x % 2
    in_vmem = pl.BlockSpec(memory_space=pltpu.VMEM)
    hbm = pl.BlockSpec(memory_space=pltpu.HBM)
    in_smem = pl.BlockSpec(memory_space=pltpu.SMEM)

    def shape(dims, dtype):
        return jax.ShapeDtypeStruct(dims, dtype)

    def in_hbm(value):
        return pltpu.with_memory_space_constraint(value, pltpu.HBM)

    wanted = [w_three, w_four.T]
    fetched = pl.pallas_call(
        fetch_kernel,
        out_shape=(shape((chan_in, held, depth), coarse.dtype),) * 3
        + tuple(shape(value.shape, value.dtype) for value in wanted),
        in_specs=[in_smem, hbm] + [hbm] * len(wanted),
        out_specs=(in_vmem,) * (3 + len(wanted)),
        scratch_shapes=(pltpu.SemaphoreType.DMA((3 + len(wanted),)),),
        compiler_params=pltpu.CompilerParams(vmem_limit_bytes=4 * MIB),
        name="fetch",
    )(at_x.reshape(1), in_hbm(coarse), *(in_hbm(value) for value in wanted))
    planes = fetched[:3]
    planes = [plane.transpose(1, 0, 2) for plane in planes]
    first_rows = jnp.stack(
        [jnp.where(core == 0, planes[i + 1][0], planes[i][0]) for i in range(2)]
    )
    rim = lax.ppermute(
        first_rows,
        ("gx", "gy"),
        [
            ((i ^ 1) * groups_y + j + 1, i * groups_y + j)
            for i in range(groups_x)
            for j in range(groups_y - 1)
        ],
    )
    part = parity_of(lax.axis_index("gx")) ^ parity_of(lax.axis_index("gy"))
    part = part.astype(jnp.int32).reshape(1)
    groups = held // 4

    def group_scratch(pairs):
        return (
            pltpu.VMEM((WINDOW, pairs * LANES), jnp.bfloat16),
            pltpu.VMEM((192, (2 * pairs + 1) * LANES), jnp.float32),
            pltpu.VMEM((LANES, pairs * LANES), jnp.bfloat16),
            pltpu.VMEM((192, (2 * pairs + 1) * LANES), jnp.bfloat16),
        )

    handed = (
        shape((fine_x, fine_y - 8, fine_z), jnp.float32),
        shape((192, 256), jnp.float32),
        shape((WINDOW, LANES), jnp.float32),
        shape((192, 256), jnp.bfloat16),
        shape((LANES, WINDOW), jnp.bfloat16),
        shape((WINDOW, LANES), jnp.bfloat16),
        shape((32, BLOCKS * LANES), jnp.bfloat16),
        shape((4, 8, fine_z), jnp.float32),
        shape((4, 8, fine_z), jnp.float32),
        shape((2, 2, 64, LANES), jnp.bfloat16),
    )
    half = shape((56, LANES), jnp.float32)
    per_group = ()
    for q in range(groups):
        per_group = per_group + group_scratch(2 if q < groups - 1 else 1)
    most, *held_back = pl.pallas_call(
        lambda *refs: interior_kernel(scale, *refs),
        out_shape=handed,
        in_specs=[in_smem] * 2 + [in_vmem] * 5 + [hbm] * 4,
        out_specs=(in_vmem,) * len(handed),
        scratch_shapes=(
            pltpu.VMEM((192, 256), jnp.float32),
            pltpu.VMEM((2, held, 64, LANES), jnp.bfloat16),
            pltpu.VMEM(elec_field.shape, jnp.bfloat16),
            pltpu.VMEM(adjoint.shape, jnp.bfloat16),
            pltpu.VMEM(temp_grad.shape, jnp.bfloat16),
            pltpu.VMEM(adjoint_grad.shape, jnp.bfloat16),
            pltpu.SemaphoreType.DMA((3, 4)),
        )
        + per_group,
        compiler_params=pltpu.CompilerParams(vmem_limit_bytes=32 * MIB),
        cost_estimate=pl.CostEstimate(
            flops=2000000000, bytes_accessed=4000000, transcendentals=2000000
        ),
        name="interior",
    )(
        core.reshape(1),
        inside,
        *planes,
        *fetched[3:],
        in_hbm(elec_field),
        in_hbm(adjoint),
        in_hbm(temp_grad),
        in_hbm(adjoint_grad),
    )
    last_dense, mine, other = pl.pallas_call(
        rim_kernel,
        out_shape=(shape((fine_x, 8, fine_z), jnp.float32), half, half),
        in_specs=[in_smem] * 2 + [in_vmem] * len(handed),
        out_specs=(in_vmem,) * 3,
        scratch_shapes=(
            pltpu.VMEM((112, LANES), jnp.float32),
            pltpu.VMEM((192, 256), jnp.float32),
            pltpu.VMEM((WINDOW, LANES), jnp.float32),
            pltpu.VMEM((2, 3, 64, LANES), jnp.bfloat16),
        )
        + group_scratch(1),
        compiler_params=pltpu.CompilerParams(vmem_limit_bytes=16 * MIB),
        cost_estimate=pl.CostEstimate(
            flops=400000000, bytes_accessed=2000000, transcendentals=400000
        ),
        name="rim",
    )(part, inside, rim, *held_back)
    density = jnp.concatenate([most, last_dense], 1)
    grad_three, grad_four = sum_everywhere(mine, other, part)
    return (density, grad_three, grad_four)


def solution(mesh):
    return jax.shard_map(
        shards,
        mesh=mesh,
        in_specs=(
            P(None, None, "gy", None),
            P(),
            P(),
            P(None, "gx", "gy", None),
            P(None, "gx", "gy", None),
            P("gx", "gy", None),
            P(None, "gx", "gy", None),
        ),
        out_specs=(P("gx", "gy", None), P(), P()),
        check_vma=False,
    )
```

```python
import math

import jax
import jax.numpy as jnp
from jax import lax
from jax.experimental import pallas as pl
from jax.experimental.pallas import tpu as pltpu
from jax.sharding import PartitionSpec as P

PAIR_ROWS = 5
BLOCKS = 3 * PAIR_ROWS * 3
WINDOW = BLOCKS * 16
LANES = 128
FRONT_APART = 7
BACK_APART = 3
MIB = 1024 * 1024


def slot_of(tap):
    tap_x, tap_y, tap_z = (tap // 9, tap // 3 % 3, tap % 3)
    off_y, off_z = (int(tap_y == 0), int(tap_z == 0))
    if tap_y == 1 and tap_z == 1:
        return (96, 32 * tap_x)
    if tap_y == 1:
        return (32 * tap_x + 16, 32 * off_z)
    if tap_z == 1:
        return (32 * tap_x + 16, 64 if off_y == 1 else 96)
    return (32 * tap_x, 64 * off_y + 32 * off_z)


def lane_index(shape):
    return lax.broadcasted_iota(jnp.int32, shape, 1)


def next_lane(tile):
    moved = pltpu.roll(tile, LANES - 1, 1)
    return jnp.where(lane_index(tile.shape) == LANES - 1, jnp.zeros_like(tile), moved)


def previous_lane(tile):
    moved = pltpu.roll(tile, 1, 1)
    return jnp.where(lane_index(tile.shape) == 0, 0.0, moved)


def logistic(values):
    return 1.0 / (1.0 + jnp.exp2(values * (-1.0 / math.log(2.0))))


def matmul(left, right):
    return jnp.dot(left, right, preferred_element_type=jnp.float32)


def matmul_nt(left, right):
    return lax.dot_general(
        left, right, (((1,), (1,)), ((), ())), preferred_element_type=jnp.float32
    )


def block_lanes(block):
    return slice(block * LANES, (block + 1) * LANES)


def fill_onehot(onehot):
    tap = lax.broadcasted_iota(jnp.int32, (32, LANES), 0)
    at = lane_index((32, LANES))
    tap_x = jnp.where(tap >= 9, 1, 0) + jnp.where(tap >= 18, 1, 0)
    within = tap - 9 * tap_x
    tap_y = jnp.where(within >= 3, 1, 0) + jnp.where(within >= 6, 1, 0)
    tap_z = within - 3 * tap_y
    twice_x = (at >> 5) + 1 - tap_x
    twice_z = ((at >> 3) & 3) + 1 - tap_z
    twice_y = (at & 7) + 1 - tap_y
    odd = (twice_x | twice_y | twice_z) & 1
    inside = jnp.minimum(jnp.minimum(twice_x, twice_y), twice_z)
    block_of = (twice_x >> 1) * 15 + (twice_y >> 1) * 3 + (twice_z >> 1)
    known = jnp.where(odd == 0, block_of, -1)
    known = jnp.where(inside >= 0, known, -1)
    known = jnp.where(tap < 27, known, -1).astype(jnp.float32).astype(jnp.bfloat16)
    one, zero = (jnp.ones((32, LANES), jnp.bfloat16), jnp.zeros((32, LANES), jnp.bfloat16))
    for block in range(BLOCKS):
        onehot[:, block_lanes(block)] = jnp.where(known == jnp.bfloat16(block), one, zero)
        if block % 5 == 4:
            yield


def fill_three(w_three, m_three, build):
    build[...] = jnp.zeros_like(build)
    for tap in range(27):
        tap_x, tap_y, tap_z = (tap // 9, tap // 3 % 3, tap % 3)
        par_y, off_y = (int(tap_y != 1), int(tap_y == 0))
        par_z, off_z = (int(tap_z != 1), int(tap_z == 0))
        row = par_y * 32 + par_z * 16
        lane = off_y * 64 + off_z * 32
        places = (((1, 1),), ((0, 0), (2, 1)), ((1, 0),))[tap_x]
        values = w_three[tap].astype(jnp.float32)
        for plane, off_x in places:
            build[
                plane * 64 + row : plane * 64 + row + 16,
                off_x * 128 + lane : off_x * 128 + lane + 32,
            ] = values
    m_three[...] = build[...].astype(jnp.bfloat16)


def fill_four(w_four, onehot, m_four, m_back):
    spread = matmul(w_four[...], onehot[:27, :])
    columns = jnp.concatenate([spread[:, block_lanes(block)] for block in range(BLOCKS)], 0)
    m_back[...] = columns.astype(jnp.bfloat16)
    m_four[...] = columns.astype(jnp.bfloat16).T


def coarse_tile(rows):
    return jnp.concatenate([rows, next_lane(rows)], 0)


def window_of(cells, b, last):
    after = b if last else b + 1
    return jnp.concatenate([cells[0, b], cells[0, after], cells[1, b], cells[1, after]], 0)


def field_pair(elec, temp, adj, adj_grad, scale, res_x, rows, lanes):
    energy = 0.0
    thermal = 0.0
    for comp in range(3):
        field = elec[comp, res_x, rows, lanes].astype(jnp.float32)
        energy = energy + field * field
        thermal = thermal + temp[comp, res_x, rows, lanes].astype(jnp.float32) * adj_grad[
            comp, res_x, rows, lanes
        ].astype(jnp.float32)
    gain = (scale * 3.0 * (1.0 - 0.001)) * (energy * adj[res_x, rows, lanes].astype(jnp.float32))
    return (gain, (scale * 2.0 * (1.0 - 0.01)) * thermal)


class Group:
    def __init__(self, pairs, first, matrices, scratch, top):
        self.pairs, self.first, self.top = (pairs, first, top)
        self.m_three, self.m_four, self.m_back = matrices
        self.cells, self.windows, self.slope, self.g_fine, self.g_pre = scratch
        self.hidden_rows = 4 * pairs + 1

    def window(self, b):
        return window_of(self.cells, self.first + b, self.top and b == 2 * self.pairs)

    def forward(self):
        coarse_rows = 2 * self.pairs + 1
        self.g_pre_blank()
        for b in range(coarse_rows):
            halo = b == coarse_rows - 1
            if halo:
                matrix = jnp.concatenate(
                    [self.m_three[plane * 64 : plane * 64 + 32, :] for plane in range(3)], 0
                )
                part = matmul(matrix, self.window(b))
            elif b % 2 == 0:
                both = matmul(
                    self.m_three[...],
                    jnp.concatenate([self.window(b), self.window(b + 1)], 1),
                )
                part = both[:, :LANES]
            else:
                part = both[:, LANES:]
            per_plane = 32 if halo else 64
            for plane in range(3):
                pre = part[plane * per_plane : (plane + 1) * per_plane]
                sigma = logistic(pre)
                hidden = pre * sigma
                self.slope[plane * 64 : plane * 64 + per_plane, block_lanes(b)] = (
                    sigma + hidden * (1.0 - sigma)
                )
                for par in range(per_plane // 32):
                    row = 2 * b + par
                    two = hidden[par * 32 : par * 32 + 32].astype(jnp.bfloat16)
                    tall = jnp.concatenate([two, next_lane(two[:16])], 0)
                    for pair in range(self.pairs):
                        within = row - 4 * pair
                        if 0 <= within < PAIR_ROWS:
                            start = (plane * PAIR_ROWS + within) * 48
                            self.windows[start : start + 48, block_lanes(pair)] = tall
                yield

    def g_pre_blank(self):
        for plane in range(3):
            self.g_pre[plane * 64 + 32 : plane * 64 + 64, block_lanes(2 * self.pairs)] = jnp.zeros(
                (32, LANES), jnp.bfloat16
            )

    def solid(self, density):
        logits = matmul(self.m_four[...], self.windows[...])
        yield
        for res_x in range(4):
            for res_z in range(4):
                at = (res_x * 4 + res_z) * 8
                density[res_x, :, block_lanes(res_z)] = logistic(
                    jnp.concatenate(
                        [logits[at : at + 8, block_lanes(pair)] for pair in range(self.pairs)], 0
                    )
                )
            yield

    def middle(self, field_terms, density):
        for res_x in range(4):
            for res_z in range(4):
                at = (res_x * 4 + res_z) * 8
                lanes = block_lanes(res_z)
                d = density[res_x, :, lanes]
                gain, loss = field_terms(res_x, lanes)
                g = d * d * (1.0 - d) * (gain * d - loss)
                if res_z % 2 == 0:
                    before = g
                    continue
                for pair in range(self.pairs):
                    rows = slice(8 * pair, 8 * pair + 8)
                    self.g_fine[at - 8 : at + 8, block_lanes(pair)] = jnp.concatenate(
                        [before[rows], g[rows]], 0
                    ).astype(jnp.bfloat16)
                yield

    def backward(self, sums_from, sums_to):
        g_out = self.g_fine[...]
        for plane in range(3):
            span = slice(plane * 240, plane * 240 + 240)
            spread = matmul(self.m_back[span, :], g_out)
            for row in range(self.hidden_rows):
                tall = 0.0
                for pair in range(self.pairs):
                    within = row - 4 * pair
                    if 0 <= within < PAIR_ROWS:
                        tall = tall + spread[within * 48 : within * 48 + 48, block_lanes(pair)]
                both = jnp.concatenate([tall[:16] + previous_lane(tall[32:]), tall[16:32]], 0)
                at = plane * 64 + row % 2 * 32
                lanes = block_lanes(row // 2)
                if plane == 1 and 0 < row < self.hidden_rows - 1:
                    both = both.astype(jnp.bfloat16).astype(jnp.float32)
                self.g_pre[at : at + 32, lanes] = (
                    both * self.slope[at : at + 32, lanes]
                ).astype(jnp.bfloat16)
            yield
            sums_to[1][span, :] = sums_from[1][span, :] + matmul_nt(self.windows[span, :], g_out)
            yield
        wide = jnp.concatenate([self.window(b) for b in range(2 * self.pairs + 1)], 1)
        sums_to[0][...] = sums_from[0][...] + matmul_nt(self.g_pre[...], wide)
        yield


def run(*streams):
    live = list(streams)
    while live:
        for entry in list(live):
            stream, count = entry
            for _ in range(count):
                if next(stream, live) is live:
                    live.remove(entry)
                    break


def staggered(pending, side, apart):
    live = []
    turn = 0
    while pending or live or side:
        if pending and turn % apart == 0:
            live.append(pending.pop(0))
        for stream in live + side[:1]:
            if next(stream, live) is live:
                (live if stream in live else side).remove(stream)
        turn = turn + 1


def chain(*streams):
    for stream in streams:
        yield from stream


def fetch_kernel(at_x, coarse, *refs):
    sems = refs[-1]
    count = (len(refs) - 4) // 2
    last = coarse.shape[1] - 1
    base = at_x[0] - lax.rem(at_x[0], 2)
    copies = [
        pltpu.make_async_copy(coarse.at[:, jnp.minimum(base + i, last), :, :], here, sems.at[i])
        for i, here in enumerate(refs[count : count + 3])
    ]
    copies = copies + [
        pltpu.make_async_copy(refs[i], refs[count + 3 + i], sems.at[3 + i]) for i in range(count)
    ]
    for copy in copies:
        copy.start()
    for copy in copies:
        copy.wait()


def interior_kernel(scale, core, inside, *refs):
    (plane_a, plane_b, plane_c, w_three, w_four, elec, adj, temp, adj_grad) = refs[:9]
    refs = refs[9:]
    (dense, sum_three, sum_four, m_three, m_four, m_back) = refs[:6]
    (onehot, last_gain, last_loss, last_cells) = refs[6:10]
    (build, cells, elec_v, adj_v, temp_v, adj_grad_v, sems) = refs[10:17]
    held = plane_a.shape[0]
    groups = held // 4
    scratch = refs[17:]
    sets = [scratch[4 * i : 4 * i + 4] for i in range(groups)]
    def copies_of(comp):
        return [
            pltpu.make_async_copy(far.at[comp], here.at[comp], sems.at[comp, i])
            for i, (far, here) in enumerate(
                ((elec, elec_v), (temp, temp_v), (adj_grad, adj_grad_v))
            )
        ]

    def start_copies(comp, carry):
        for copy in copies_of(comp):
            copy.start()
        return carry

    adjoint_copy = pltpu.make_async_copy(adj, adj_v, sems.at[0, 3])
    adjoint_copy.start()
    lax.fori_loop(0, 3, start_copies, 0)

    def field_terms_at(first, count):
        rows = slice(first, first + count)
        return lambda res_x, lanes: field_pair(
            elec_v, temp_v, adj_v, adj_grad_v, scale, res_x, rows, lanes
        )

    known = inside[0].astype(jnp.float32).astype(jnp.bfloat16)

    def load_cells():
        low = core[0] == 0
        for b in range(held):
            near = jnp.where(low, plane_a[b], plane_b[b])
            far = known * jnp.where(low, plane_b[b], plane_c[b])
            for plane, rows in enumerate((near, far)):
                tile = coarse_tile(rows)
                cells[plane, b] = tile
                if b >= held - 2:
                    last_cells[plane, b - held + 2] = tile
            yield

    def zero_sums():
        sum_three[...] = jnp.zeros_like(sum_three)
        yield
        sum_four[...] = jnp.zeros_like(sum_four)
        yield

    matrices = (m_three, m_four, m_back)
    sums = (sum_three, sum_four)
    parts = []
    for q in range(groups):
        pairs = 2 if q < groups - 1 else 1
        parts.append(Group(pairs, 4 * q, matrices, (cells,) + tuple(sets[q]), False))

    def front(q):
        yield from parts[q].forward()
        yield from parts[q].solid(dense.at[:, rows_of(q), :])

    def back(q):
        yield from parts[q].middle(
            field_terms_at(16 * q, 8 * parts[q].pairs), dense.at[:, rows_of(q), :]
        )
        yield from parts[q].backward(sums, sums)

    def rows_of(q):
        return slice(16 * q, 16 * q + 8 * parts[q].pairs)

    def last_fields():
        terms = field_terms_at(16 * groups - 8, 8)
        for res_x in range(4):
            for res_z in range(4):
                lanes = block_lanes(res_z)
                gain, loss = terms(res_x, lanes)
                last_gain[res_x, :, lanes] = gain
                last_loss[res_x, :, lanes] = loss
            yield

    run((fill_onehot(onehot), 1), (load_cells(), 2), (zero_sums(), 1))
    fill_four(w_four, onehot, m_four, m_back)
    fill_three(w_three, m_three, build)
    staggered([front(q) for q in range(groups)], [], FRONT_APART)
    adjoint_copy.wait()
    for comp in range(3):
        for copy in copies_of(comp):
            copy.wait()
    staggered([back(q) for q in range(groups)], [last_fields()], BACK_APART)


def rim_kernel(part, inside, rim, sum_three_in, sum_four_in, *refs):
    (m_three, m_four, m_back, onehot, last_gain, last_loss, last_cells) = refs[:7]
    (dense, mine, other) = refs[7:10]
    (packed, sum_three, sum_four, cells) = refs[10:14]
    scratch = refs[14:]
    known = inside[0].astype(jnp.float32).astype(jnp.bfloat16)
    for plane in range(2):
        for b in range(2):
            cells[plane, b] = last_cells[plane, b]
        cells[plane, 2] = coarse_tile(rim[plane] if plane == 0 else known * rim[plane])
    group = Group(1, 0, (m_three, m_four, m_back), (cells,) + tuple(scratch), True)
    run((group.forward(), 1))
    terms = lambda res_x, lanes: (last_gain[res_x, :, lanes], last_loss[res_x, :, lanes])
    run((group.solid(dense), 1))
    run((group.middle(terms, dense), 1))
    run((group.backward((sum_three_in, sum_four_in), (sum_three, sum_four)), 1))
    by_tap = (
        sum_three[64:128, 128:],
        sum_three[:64, :128] + sum_three[128:, 128:],
        sum_three[64:128, :128],
    )
    for tap_x in range(3):
        along = by_tap[tap_x]
        packed[32 * tap_x : 32 * tap_x + 16, :] = along[48:64]
        lanes = lane_index((16, LANES))
        mixed = jnp.where(
            lanes < 64,
            along[16:32],
            jnp.where(lanes < 96, along[32:48], pltpu.roll(along[32:48], 96, 1)),
        )
        packed[32 * tap_x + 16 : 32 * tap_x + 32, :] = mixed
        packed[96:112, 32 * tap_x : 32 * tap_x + 32] = along[:16, :32]
    rest = jnp.concatenate(
        [sum_four[16 * block : 16 * block + 16, :] for block in range(BLOCKS)], 1
    )
    pieces = []
    for _ in range(3):
        piece = rest.astype(jnp.bfloat16)
        pieces.append(piece)
        rest = rest - piece.astype(jnp.float32)
    folded = matmul_nt(jnp.concatenate(pieces, 0), onehot[...])
    packed[96:112, 96:128] = folded[:16] + folded[16:32] + folded[32:48]
    which = part[0]
    half = mine.shape[0]
    mine[...] = packed[pl.ds(pl.multiple_of(which * half, 8), half), :]
    other[...] = packed[pl.ds(pl.multiple_of((1 - which) * half, 8), half), :]


def unpack_kernel(part, mine, other, grad_three, grad_four):
    low = part[0] == 0
    whole = jnp.concatenate(
        [
            jnp.where(low, mine[...], other[...]),
            jnp.where(low, other[...], mine[...]),
        ],
        0,
    )
    for tap in range(27):
        row, lane = slot_of(tap)
        grad_three[tap] = whole[row : row + 16, lane : lane + 32]
    grad_four[...] = whole[96:112, 96:123]


def exchanged(value, bit_x, bit_y):
    size_x, size_y = (lax.axis_size("gx"), lax.axis_size("gy"))
    pairs = [
        (i * size_y + j, (i ^ bit_x) * size_y + (j ^ bit_y))
        for i in range(size_x)
        for j in range(size_y)
    ]
    return lax.ppermute(value, ("gx", "gy"), pairs)


def parity_of(index):
    total = index
    for shift in (1, 2, 3, 4, 5, 6, 7):
        total = total ^ (index >> shift)
    return total & 1


def sum_everywhere(mine, other, part):
    size_x, size_y = (lax.axis_size("gx"), lax.axis_size("gy"))
    assert size_x & (size_x - 1) == 0 and size_y & (size_y - 1) == 0
    assert 2 <= size_x <= 256 and size_y <= 256
    mine = mine + exchanged(other, 1, 0)
    bit = 2
    while bit < size_x:
        mine = mine + exchanged(mine, bit + 1, 0)
        bit = bit * 2
    bit = 1
    while bit < size_y:
        mine = mine + exchanged(mine, 1, bit)
        bit = bit * 2
    other = exchanged(mine, 1, 0)
    spec = pl.BlockSpec(memory_space=pltpu.VMEM)
    grad_three, grad_four = pl.pallas_call(
        unpack_kernel,
        out_shape=(
            jax.ShapeDtypeStruct((27, 16, 32), jnp.float32),
            jax.ShapeDtypeStruct((16, 27), jnp.float32),
        ),
        in_specs=[pl.BlockSpec(memory_space=pltpu.SMEM), spec, spec],
        out_specs=(spec, spec),
        compiler_params=pltpu.CompilerParams(vmem_limit_bytes=2 * MIB),
        name="unpack",
    )(part, mine, other)
    return (grad_three, grad_four.T)


def shards(coarse, w_three, w_four, elec_field, temp_grad, adjoint, adjoint_grad):
    groups_x, groups_y = (lax.axis_size("gx"), lax.axis_size("gy"))
    chan_in, count_a, held, depth = coarse.shape
    fine_x, fine_y, fine_z = adjoint.shape
    assert (fine_x, fine_y, fine_z) == (4, 4 * held, 4 * LANES)
    assert depth == LANES and chan_in == 32 and held % 4 == 0 and count_a == groups_x
    cells = fine_x * groups_x * fine_y * groups_y * fine_z
    scale = 8.0 / math.sqrt(cells)
    at_x = lax.axis_index("gx").astype(jnp.int32)
    inside = (at_x + 1 < count_a).astype(jnp.int32).reshape(1)
    core = at_x % 2
    in_vmem = pl.BlockSpec(memory_space=pltpu.VMEM)
    hbm = pl.BlockSpec(memory_space=pltpu.HBM)
    in_smem = pl.BlockSpec(memory_space=pltpu.SMEM)

    def shape(dims, dtype):
        return jax.ShapeDtypeStruct(dims, dtype)

    def in_hbm(value):
        return pltpu.with_memory_space_constraint(value, pltpu.HBM)

    wanted = [w_three, w_four.T]
    fetched = pl.pallas_call(
        fetch_kernel,
        out_shape=(shape((chan_in, held, depth), coarse.dtype),) * 3
        + tuple(shape(value.shape, value.dtype) for value in wanted),
        in_specs=[in_smem, hbm] + [hbm] * len(wanted),
        out_specs=(in_vmem,) * (3 + len(wanted)),
        scratch_shapes=(pltpu.SemaphoreType.DMA((3 + len(wanted),)),),
        compiler_params=pltpu.CompilerParams(vmem_limit_bytes=4 * MIB),
        name="fetch",
    )(at_x.reshape(1), in_hbm(coarse), *(in_hbm(value) for value in wanted))
    planes = fetched[:3]
    planes = [plane.transpose(1, 0, 2) for plane in planes]
    first_rows = jnp.stack(
        [jnp.where(core == 0, planes[i + 1][0], planes[i][0]) for i in range(2)]
    )
    rim = lax.ppermute(
        first_rows,
        ("gx", "gy"),
        [
            ((i ^ 1) * groups_y + j + 1, i * groups_y + j)
            for i in range(groups_x)
            for j in range(groups_y - 1)
        ],
    )
    part = parity_of(lax.axis_index("gx")) ^ parity_of(lax.axis_index("gy"))
    part = part.astype(jnp.int32).reshape(1)
    groups = held // 4

    def group_scratch(pairs):
        return (
            pltpu.VMEM((WINDOW, pairs * LANES), jnp.bfloat16),
            pltpu.VMEM((192, (2 * pairs + 1) * LANES), jnp.float32),
            pltpu.VMEM((LANES, pairs * LANES), jnp.bfloat16),
            pltpu.VMEM((192, (2 * pairs + 1) * LANES), jnp.bfloat16),
        )

    handed = (
        shape((fine_x, fine_y - 8, fine_z), jnp.float32),
        shape((192, 256), jnp.float32),
        shape((WINDOW, LANES), jnp.float32),
        shape((192, 256), jnp.bfloat16),
        shape((LANES, WINDOW), jnp.bfloat16),
        shape((WINDOW, LANES), jnp.bfloat16),
        shape((32, BLOCKS * LANES), jnp.bfloat16),
        shape((4, 8, fine_z), jnp.float32),
        shape((4, 8, fine_z), jnp.float32),
        shape((2, 2, 64, LANES), jnp.bfloat16),
    )
    half = shape((56, LANES), jnp.float32)
    per_group = ()
    for q in range(groups):
        per_group = per_group + group_scratch(2 if q < groups - 1 else 1)
    most, *held_back = pl.pallas_call(
        lambda *refs: interior_kernel(scale, *refs),
        out_shape=handed,
        in_specs=[in_smem] * 2 + [in_vmem] * 5 + [hbm] * 4,
        out_specs=(in_vmem,) * len(handed),
        scratch_shapes=(
            pltpu.VMEM((192, 256), jnp.float32),
            pltpu.VMEM((2, held, 64, LANES), jnp.bfloat16),
            pltpu.VMEM(elec_field.shape, jnp.bfloat16),
            pltpu.VMEM(adjoint.shape, jnp.bfloat16),
            pltpu.VMEM(temp_grad.shape, jnp.bfloat16),
            pltpu.VMEM(adjoint_grad.shape, jnp.bfloat16),
            pltpu.SemaphoreType.DMA((3, 4)),
        )
        + per_group,
        compiler_params=pltpu.CompilerParams(vmem_limit_bytes=32 * MIB),
        cost_estimate=pl.CostEstimate(
            flops=2000000000, bytes_accessed=4000000, transcendentals=2000000
        ),
        name="interior",
    )(
        core.reshape(1),
        inside,
        *planes,
        *fetched[3:],
        in_hbm(elec_field),
        in_hbm(adjoint),
        in_hbm(temp_grad),
        in_hbm(adjoint_grad),
    )
    last_dense, mine, other = pl.pallas_call(
        rim_kernel,
        out_shape=(shape((fine_x, 8, fine_z), jnp.float32), half, half),
        in_specs=[in_smem] * 2 + [in_vmem] * len(handed),
        out_specs=(in_vmem,) * 3,
        scratch_shapes=(
            pltpu.VMEM((112, LANES), jnp.float32),
            pltpu.VMEM((192, 256), jnp.float32),
            pltpu.VMEM((WINDOW, LANES), jnp.float32),
            pltpu.VMEM((2, 3, 64, LANES), jnp.bfloat16),
        )
        + group_scratch(1),
        compiler_params=pltpu.CompilerParams(vmem_limit_bytes=16 * MIB),
        cost_estimate=pl.CostEstimate(
            flops=400000000, bytes_accessed=2000000, transcendentals=400000
        ),
        name="rim",
    )(part, inside, rim, *held_back)
    density = jnp.concatenate([most, last_dense], 1)
    grad_three, grad_four = sum_everywhere(mine, other, part)
    return (density, grad_three, grad_four)


def solution(mesh):
    return jax.shard_map(
        shards,
        mesh=mesh,
        in_specs=(
            P(None, None, "gy", None),
            P(),
            P(),
            P(None, "gx", "gy", None),
            P(None, "gx", "gy", None),
            P("gx", "gy", None),
            P(None, "gx", "gy", None),
        ),
        out_specs=(P("gx", "gy", None), P(), P()),
        check_vma=False,
    )
```

```python
import math

import jax
import jax.numpy as jnp
from jax import lax
from jax.experimental import pallas as pl
from jax.experimental.pallas import tpu as pltpu
from jax.sharding import PartitionSpec as P

PAIR_ROWS = 5
BLOCKS = 3 * PAIR_ROWS * 3
WINDOW = BLOCKS * 16
LANES = 128
FRONT_APART = 7
BACK_APART = 3
MIB = 1024 * 1024


def slot_of(tap):
    tap_x, tap_y, tap_z = (tap // 9, tap // 3 % 3, tap % 3)
    off_y, off_z = (int(tap_y == 0), int(tap_z == 0))
    if tap_y == 1 and tap_z == 1:
        return (96, 32 * tap_x)
    if tap_y == 1:
        return (32 * tap_x + 16, 32 * off_z)
    if tap_z == 1:
        return (32 * tap_x + 16, 64 if off_y == 1 else 96)
    return (32 * tap_x, 64 * off_y + 32 * off_z)


def lane_index(shape):
    return lax.broadcasted_iota(jnp.int32, shape, 1)


def next_lane(tile):
    moved = pltpu.roll(tile, LANES - 1, 1)
    return jnp.where(lane_index(tile.shape) == LANES - 1, jnp.zeros_like(tile), moved)


def previous_lane(tile):
    moved = pltpu.roll(tile, 1, 1)
    return jnp.where(lane_index(tile.shape) == 0, 0.0, moved)


def logistic(values):
    return 1.0 / (1.0 + jnp.exp2(values * (-1.0 / math.log(2.0))))


def matmul(left, right):
    return jnp.dot(left, right, preferred_element_type=jnp.float32)


def matmul_nt(left, right):
    return lax.dot_general(
        left, right, (((1,), (1,)), ((), ())), preferred_element_type=jnp.float32
    )


def block_lanes(block):
    return slice(block * LANES, (block + 1) * LANES)


def fill_onehot(onehot):
    tap = lax.broadcasted_iota(jnp.int32, (32, LANES), 0)
    at = lane_index((32, LANES))
    tap_x = jnp.where(tap >= 9, 1, 0) + jnp.where(tap >= 18, 1, 0)
    within = tap - 9 * tap_x
    tap_y = jnp.where(within >= 3, 1, 0) + jnp.where(within >= 6, 1, 0)
    tap_z = within - 3 * tap_y
    twice_x = (at >> 5) + 1 - tap_x
    twice_z = ((at >> 3) & 3) + 1 - tap_z
    twice_y = (at & 7) + 1 - tap_y
    odd = (twice_x | twice_y | twice_z) & 1
    inside = jnp.minimum(jnp.minimum(twice_x, twice_y), twice_z)
    block_of = (twice_x >> 1) * 15 + (twice_y >> 1) * 3 + (twice_z >> 1)
    known = jnp.where(odd == 0, block_of, -1)
    known = jnp.where(inside >= 0, known, -1)
    known = jnp.where(tap < 27, known, -1).astype(jnp.float32).astype(jnp.bfloat16)
    one, zero = (jnp.ones((32, LANES), jnp.bfloat16), jnp.zeros((32, LANES), jnp.bfloat16))
    for block in range(BLOCKS):
        onehot[:, block_lanes(block)] = jnp.where(known == jnp.bfloat16(block), one, zero)
        if block % 5 == 4:
            yield


def fill_three(w_three, m_three, build):
    build[...] = jnp.zeros_like(build)
    for tap in range(27):
        tap_x, tap_y, tap_z = (tap // 9, tap // 3 % 3, tap % 3)
        par_y, off_y = (int(tap_y != 1), int(tap_y == 0))
        par_z, off_z = (int(tap_z != 1), int(tap_z == 0))
        row = par_y * 32 + par_z * 16
        lane = off_y * 64 + off_z * 32
        places = (((1, 1),), ((0, 0), (2, 1)), ((1, 0),))[tap_x]
        values = w_three[tap].astype(jnp.float32)
        for plane, off_x in places:
            build[
                plane * 64 + row : plane * 64 + row + 16,
                off_x * 128 + lane : off_x * 128 + lane + 32,
            ] = values
    m_three[...] = build[...].astype(jnp.bfloat16)


def fill_four(w_four, onehot, m_four, m_back):
    spread = matmul(w_four[...], onehot[:27, :])
    columns = jnp.concatenate([spread[:, block_lanes(block)] for block in range(BLOCKS)], 0)
    m_back[...] = columns.astype(jnp.bfloat16)
    m_four[...] = columns.astype(jnp.bfloat16).T


def coarse_tile(rows):
    return jnp.concatenate([rows, next_lane(rows)], 0)


def window_of(cells, b, last):
    after = b if last else b + 1
    return jnp.concatenate([cells[0, b], cells[0, after], cells[1, b], cells[1, after]], 0)


def field_pair(elec, temp, adj, adj_grad, scale, res_x, rows, lanes):
    energy = 0.0
    thermal = 0.0
    for comp in range(3):
        field = elec[comp, res_x, rows, lanes].astype(jnp.float32)
        energy = energy + field * field
        thermal = thermal + temp[comp, res_x, rows, lanes].astype(jnp.float32) * adj_grad[
            comp, res_x, rows, lanes
        ].astype(jnp.float32)
    gain = (scale * 3.0 * (1.0 - 0.001)) * (energy * adj[res_x, rows, lanes].astype(jnp.float32))
    return (gain, (scale * 2.0 * (1.0 - 0.01)) * thermal)


class Group:
    def __init__(self, pairs, first, matrices, scratch, top):
        self.pairs, self.first, self.top = (pairs, first, top)
        self.m_three, self.m_four, self.m_back = matrices
        self.cells, self.windows, self.slope, self.g_fine, self.g_pre = scratch
        self.hidden_rows = 4 * pairs + 1

    def window(self, b):
        return window_of(self.cells, self.first + b, self.top and b == 2 * self.pairs)

    def forward(self):
        coarse_rows = 2 * self.pairs + 1
        self.g_pre_blank()
        for b in range(coarse_rows):
            halo = b == coarse_rows - 1
            if halo:
                matrix = jnp.concatenate(
                    [self.m_three[plane * 64 : plane * 64 + 32, :] for plane in range(3)], 0
                )
                part = matmul(matrix, self.window(b))
            elif b % 2 == 0:
                both = matmul(
                    self.m_three[...],
                    jnp.concatenate([self.window(b), self.window(b + 1)], 1),
                )
                part = both[:, :LANES]
            else:
                part = both[:, LANES:]
            per_plane = 32 if halo else 64
            for plane in range(3):
                pre = part[plane * per_plane : (plane + 1) * per_plane]
                sigma = logistic(pre)
                hidden = pre * sigma
                self.slope[plane * 64 : plane * 64 + per_plane, block_lanes(b)] = (
                    sigma + hidden * (1.0 - sigma)
                )
                for par in range(per_plane // 32):
                    row = 2 * b + par
                    two = hidden[par * 32 : par * 32 + 32].astype(jnp.bfloat16)
                    tall = jnp.concatenate([two, next_lane(two[:16])], 0)
                    for pair in range(self.pairs):
                        within = row - 4 * pair
                        if 0 <= within < PAIR_ROWS:
                            start = (plane * PAIR_ROWS + within) * 48
                            self.windows[start : start + 48, block_lanes(pair)] = tall
                yield

    def g_pre_blank(self):
        for plane in range(3):
            self.g_pre[plane * 64 + 32 : plane * 64 + 64, block_lanes(2 * self.pairs)] = jnp.zeros(
                (32, LANES), jnp.bfloat16
            )

    def solid(self, density):
        logits = matmul(self.m_four[...], self.windows[...])
        yield
        for res_x in range(4):
            for res_z in range(4):
                at = (res_x * 4 + res_z) * 8
                density[res_x, :, block_lanes(res_z)] = logistic(
                    jnp.concatenate(
                        [logits[at : at + 8, block_lanes(pair)] for pair in range(self.pairs)], 0
                    )
                )
            yield

    def middle(self, field_terms, density):
        for res_x in range(4):
            for res_z in range(4):
                at = (res_x * 4 + res_z) * 8
                lanes = block_lanes(res_z)
                d = density[res_x, :, lanes]
                gain, loss = field_terms(res_x, lanes)
                g = d * d * (1.0 - d) * (gain * d - loss)
                if res_z % 2 == 0:
                    before = g
                    continue
                for pair in range(self.pairs):
                    rows = slice(8 * pair, 8 * pair + 8)
                    self.g_fine[at - 8 : at + 8, block_lanes(pair)] = jnp.concatenate(
                        [before[rows], g[rows]], 0
                    ).astype(jnp.bfloat16)
                yield

    def backward(self, sums_from, sums_to):
        g_out = self.g_fine[...]
        for plane in range(3):
            span = slice(plane * 240, plane * 240 + 240)
            spread = matmul(self.m_back[span, :], g_out)
            for row in range(self.hidden_rows):
                tall = 0.0
                for pair in range(self.pairs):
                    within = row - 4 * pair
                    if 0 <= within < PAIR_ROWS:
                        tall = tall + spread[within * 48 : within * 48 + 48, block_lanes(pair)]
                both = jnp.concatenate([tall[:16] + previous_lane(tall[32:]), tall[16:32]], 0)
                at = plane * 64 + row % 2 * 32
                lanes = block_lanes(row // 2)
                if plane == 1 and 0 < row < self.hidden_rows - 1:
                    both = both.astype(jnp.bfloat16).astype(jnp.float32)
                self.g_pre[at : at + 32, lanes] = (
                    both * self.slope[at : at + 32, lanes]
                ).astype(jnp.bfloat16)
            yield
            part = matmul_nt(self.windows[span, :], g_out)
            sums_to[1][span, :] = part if sums_from is None else sums_from[1][span, :] + part
            yield
        wide = jnp.concatenate([self.window(b) for b in range(2 * self.pairs + 1)], 1)
        part = matmul_nt(self.g_pre[...], wide)
        sums_to[0][...] = part if sums_from is None else sums_from[0][...] + part
        yield


def run(*streams):
    live = list(streams)
    while live:
        for entry in list(live):
            stream, count = entry
            for _ in range(count):
                if next(stream, live) is live:
                    live.remove(entry)
                    break


def staggered(pending, side, apart):
    live = []
    turn = 0
    while pending or live or side:
        if pending and turn % apart == 0:
            live.append(pending.pop(0))
        for stream in live + side[:1]:
            if next(stream, live) is live:
                (live if stream in live else side).remove(stream)
        turn = turn + 1


def chain(*streams):
    for stream in streams:
        yield from stream


def fetch_kernel(at_x, coarse, *refs):
    sems = refs[-1]
    count = (len(refs) - 4) // 2
    last = coarse.shape[1] - 1
    base = at_x[0] - lax.rem(at_x[0], 2)
    copies = [
        pltpu.make_async_copy(coarse.at[:, jnp.minimum(base + i, last), :, :], here, sems.at[i])
        for i, here in enumerate(refs[count : count + 3])
    ]
    copies = copies + [
        pltpu.make_async_copy(refs[i], refs[count + 3 + i], sems.at[3 + i]) for i in range(count)
    ]
    for copy in copies:
        copy.start()
    for copy in copies:
        copy.wait()


def interior_kernel(scale, core, inside, *refs):
    (plane_a, plane_b, plane_c, w_three, w_four, elec, adj, temp, adj_grad) = refs[:9]
    refs = refs[9:]
    (dense, sum_three, sum_four, m_three, m_four, m_back) = refs[:6]
    (onehot, last_gain, last_loss, last_cells) = refs[6:10]
    (build, cells, elec_v, adj_v, temp_v, adj_grad_v, sems) = refs[10:17]
    held = plane_a.shape[0]
    groups = held // 4
    scratch = refs[17:]
    sets = [scratch[4 * i : 4 * i + 4] for i in range(groups)]
    def copies_of(comp):
        return [
            pltpu.make_async_copy(far.at[comp], here.at[comp], sems.at[comp, i])
            for i, (far, here) in enumerate(
                ((elec, elec_v), (temp, temp_v), (adj_grad, adj_grad_v))
            )
        ]

    def start_copies(comp, carry):
        for copy in copies_of(comp):
            copy.start()
        return carry

    adjoint_copy = pltpu.make_async_copy(adj, adj_v, sems.at[0, 3])
    adjoint_copy.start()
    lax.fori_loop(0, 3, start_copies, 0)

    def field_terms_at(first, count):
        rows = slice(first, first + count)
        return lambda res_x, lanes: field_pair(
            elec_v, temp_v, adj_v, adj_grad_v, scale, res_x, rows, lanes
        )

    known = inside[0].astype(jnp.float32).astype(jnp.bfloat16)

    def load_cells():
        low = core[0] == 0
        for b in range(held):
            near = jnp.where(low, plane_a[b], plane_b[b])
            far = known * jnp.where(low, plane_b[b], plane_c[b])
            for plane, rows in enumerate((near, far)):
                tile = coarse_tile(rows)
                cells[plane, b] = tile
                if b >= held - 2:
                    last_cells[plane, b - held + 2] = tile
            yield

    matrices = (m_three, m_four, m_back)
    sums = (sum_three, sum_four)
    parts = []
    for q in range(groups):
        pairs = 2 if q < groups - 1 else 1
        parts.append(Group(pairs, 4 * q, matrices, (cells,) + tuple(sets[q]), False))

    def front(q):
        yield from parts[q].forward()
        yield from parts[q].solid(dense.at[:, rows_of(q), :])

    def back(q):
        yield from parts[q].middle(
            field_terms_at(16 * q, 8 * parts[q].pairs), dense.at[:, rows_of(q), :]
        )
        yield from parts[q].backward(sums if q > 0 else None, sums)

    def rows_of(q):
        return slice(16 * q, 16 * q + 8 * parts[q].pairs)

    def last_fields():
        terms = field_terms_at(16 * groups - 8, 8)
        for res_x in range(4):
            for res_z in range(4):
                lanes = block_lanes(res_z)
                gain, loss = terms(res_x, lanes)
                last_gain[res_x, :, lanes] = gain
                last_loss[res_x, :, lanes] = loss
            yield

    run((fill_onehot(onehot), 1), (load_cells(), 2))
    fill_four(w_four, onehot, m_four, m_back)
    fill_three(w_three, m_three, build)
    staggered([front(q) for q in range(groups)], [], FRONT_APART)
    adjoint_copy.wait()
    for comp in range(3):
        for copy in copies_of(comp):
            copy.wait()
    staggered([back(q) for q in range(groups)], [last_fields()], BACK_APART)


def rim_kernel(part, inside, rim, sum_three_in, sum_four_in, *refs):
    (m_three, m_four, m_back, onehot, last_gain, last_loss, last_cells) = refs[:7]
    (dense, mine, other) = refs[7:10]
    (packed, sum_three, sum_four, cells) = refs[10:14]
    scratch = refs[14:]
    known = inside[0].astype(jnp.float32).astype(jnp.bfloat16)
    for plane in range(2):
        for b in range(2):
            cells[plane, b] = last_cells[plane, b]
        cells[plane, 2] = coarse_tile(rim[plane] if plane == 0 else known * rim[plane])
    group = Group(1, 0, (m_three, m_four, m_back), (cells,) + tuple(scratch), True)
    run((group.forward(), 1))
    terms = lambda res_x, lanes: (last_gain[res_x, :, lanes], last_loss[res_x, :, lanes])
    run((group.solid(dense), 1))
    run((group.middle(terms, dense), 1))
    run((group.backward((sum_three_in, sum_four_in), (sum_three, sum_four)), 1))
    by_tap = (
        sum_three[64:128, 128:],
        sum_three[:64, :128] + sum_three[128:, 128:],
        sum_three[64:128, :128],
    )
    for tap_x in range(3):
        along = by_tap[tap_x]
        packed[32 * tap_x : 32 * tap_x + 16, :] = along[48:64]
        lanes = lane_index((16, LANES))
        mixed = jnp.where(
            lanes < 64,
            along[16:32],
            jnp.where(lanes < 96, along[32:48], pltpu.roll(along[32:48], 96, 1)),
        )
        packed[32 * tap_x + 16 : 32 * tap_x + 32, :] = mixed
        packed[96:112, 32 * tap_x : 32 * tap_x + 32] = along[:16, :32]
    rest = jnp.concatenate(
        [sum_four[16 * block : 16 * block + 16, :] for block in range(BLOCKS)], 1
    )
    pieces = []
    for _ in range(3):
        piece = rest.astype(jnp.bfloat16)
        pieces.append(piece)
        rest = rest - piece.astype(jnp.float32)
    folded = matmul_nt(jnp.concatenate(pieces, 0), onehot[...])
    packed[96:112, 96:128] = folded[:16] + folded[16:32] + folded[32:48]
    which = part[0]
    half = mine.shape[0]
    mine[...] = packed[pl.ds(pl.multiple_of(which * half, 8), half), :]
    other[...] = packed[pl.ds(pl.multiple_of((1 - which) * half, 8), half), :]


def unpack_kernel(part, mine, other, grad_three, grad_four):
    low = part[0] == 0
    whole = jnp.concatenate(
        [
            jnp.where(low, mine[...], other[...]),
            jnp.where(low, other[...], mine[...]),
        ],
        0,
    )
    for tap in range(27):
        row, lane = slot_of(tap)
        grad_three[tap] = whole[row : row + 16, lane : lane + 32]
    grad_four[...] = whole[96:112, 96:123]


def exchanged(value, bit_x, bit_y):
    size_x, size_y = (lax.axis_size("gx"), lax.axis_size("gy"))
    pairs = [
        (i * size_y + j, (i ^ bit_x) * size_y + (j ^ bit_y))
        for i in range(size_x)
        for j in range(size_y)
    ]
    return lax.ppermute(value, ("gx", "gy"), pairs)


def parity_of(index):
    total = index
    for shift in (1, 2, 3, 4, 5, 6, 7):
        total = total ^ (index >> shift)
    return total & 1


def sum_everywhere(mine, other, part):
    size_x, size_y = (lax.axis_size("gx"), lax.axis_size("gy"))
    assert size_x & (size_x - 1) == 0 and size_y & (size_y - 1) == 0
    assert 2 <= size_x <= 256 and size_y <= 256
    mine = mine + exchanged(other, 1, 0)
    bit = 1
    while bit < size_y:
        mine = mine + exchanged(mine, 1, bit)
        bit = bit * 2
    bit = 2
    while bit < size_x:
        mine = mine + exchanged(mine, bit + 1, 0)
        bit = bit * 2
    other = exchanged(mine, 1, 0)
    spec = pl.BlockSpec(memory_space=pltpu.VMEM)
    grad_three, grad_four = pl.pallas_call(
        unpack_kernel,
        out_shape=(
            jax.ShapeDtypeStruct((27, 16, 32), jnp.float32),
            jax.ShapeDtypeStruct((16, 27), jnp.float32),
        ),
        in_specs=[pl.BlockSpec(memory_space=pltpu.SMEM), spec, spec],
        out_specs=(spec, spec),
        compiler_params=pltpu.CompilerParams(vmem_limit_bytes=2 * MIB),
        name="unpack",
    )(part, mine, other)
    return (grad_three, grad_four.T)


def shards(coarse, w_three, w_four, elec_field, temp_grad, adjoint, adjoint_grad):
    groups_x, groups_y = (lax.axis_size("gx"), lax.axis_size("gy"))
    chan_in, count_a, held, depth = coarse.shape
    fine_x, fine_y, fine_z = adjoint.shape
    assert (fine_x, fine_y, fine_z) == (4, 4 * held, 4 * LANES)
    assert depth == LANES and chan_in == 32 and held % 4 == 0 and count_a == groups_x
    cells = fine_x * groups_x * fine_y * groups_y * fine_z
    scale = 8.0 / math.sqrt(cells)
    at_x = lax.axis_index("gx").astype(jnp.int32)
    inside = (at_x + 1 < count_a).astype(jnp.int32).reshape(1)
    core = at_x % 2
    in_vmem = pl.BlockSpec(memory_space=pltpu.VMEM)
    hbm = pl.BlockSpec(memory_space=pltpu.HBM)
    in_smem = pl.BlockSpec(memory_space=pltpu.SMEM)

    def shape(dims, dtype):
        return jax.ShapeDtypeStruct(dims, dtype)

    def in_hbm(value):
        return pltpu.with_memory_space_constraint(value, pltpu.HBM)

    wanted = [w_three, w_four.T]
    fetched = pl.pallas_call(
        fetch_kernel,
        out_shape=(shape((chan_in, held, depth), coarse.dtype),) * 3
        + tuple(shape(value.shape, value.dtype) for value in wanted),
        in_specs=[in_smem, hbm] + [hbm] * len(wanted),
        out_specs=(in_vmem,) * (3 + len(wanted)),
        scratch_shapes=(pltpu.SemaphoreType.DMA((3 + len(wanted),)),),
        compiler_params=pltpu.CompilerParams(vmem_limit_bytes=4 * MIB),
        name="fetch",
    )(at_x.reshape(1), in_hbm(coarse), *(in_hbm(value) for value in wanted))
    planes = fetched[:3]
    planes = [plane.transpose(1, 0, 2) for plane in planes]
    first_rows = jnp.stack(
        [jnp.where(core == 0, planes[i + 1][0], planes[i][0]) for i in range(2)]
    )
    rim = lax.ppermute(
        first_rows,
        ("gx", "gy"),
        [
            ((i ^ 1) * groups_y + j + 1, i * groups_y + j)
            for i in range(groups_x)
            for j in range(groups_y - 1)
        ],
    )
    part = parity_of(lax.axis_index("gx")) ^ parity_of(lax.axis_index("gy"))
    part = part.astype(jnp.int32).reshape(1)
    groups = held // 4

    def group_scratch(pairs):
        return (
            pltpu.VMEM((WINDOW, pairs * LANES), jnp.bfloat16),
            pltpu.VMEM((192, (2 * pairs + 1) * LANES), jnp.float32),
            pltpu.VMEM((LANES, pairs * LANES), jnp.bfloat16),
            pltpu.VMEM((192, (2 * pairs + 1) * LANES), jnp.bfloat16),
        )

    handed = (
        shape((fine_x, fine_y - 8, fine_z), jnp.float32),
        shape((192, 256), jnp.float32),
        shape((WINDOW, LANES), jnp.float32),
        shape((192, 256), jnp.bfloat16),
        shape((LANES, WINDOW), jnp.bfloat16),
        shape((WINDOW, LANES), jnp.bfloat16),
        shape((32, BLOCKS * LANES), jnp.bfloat16),
        shape((4, 8, fine_z), jnp.float32),
        shape((4, 8, fine_z), jnp.float32),
        shape((2, 2, 64, LANES), jnp.bfloat16),
    )
    half = shape((56, LANES), jnp.float32)
    per_group = ()
    for q in range(groups):
        per_group = per_group + group_scratch(2 if q < groups - 1 else 1)
    most, *held_back = pl.pallas_call(
        lambda *refs: interior_kernel(scale, *refs),
        out_shape=handed,
        in_specs=[in_smem] * 2 + [in_vmem] * 5 + [hbm] * 4,
        out_specs=(in_vmem,) * len(handed),
        scratch_shapes=(
            pltpu.VMEM((192, 256), jnp.float32),
            pltpu.VMEM((2, held, 64, LANES), jnp.bfloat16),
            pltpu.VMEM(elec_field.shape, jnp.bfloat16),
            pltpu.VMEM(adjoint.shape, jnp.bfloat16),
            pltpu.VMEM(temp_grad.shape, jnp.bfloat16),
            pltpu.VMEM(adjoint_grad.shape, jnp.bfloat16),
            pltpu.SemaphoreType.DMA((3, 4)),
        )
        + per_group,
        compiler_params=pltpu.CompilerParams(vmem_limit_bytes=32 * MIB),
        cost_estimate=pl.CostEstimate(
            flops=2000000000, bytes_accessed=4000000, transcendentals=2000000
        ),
        name="interior",
    )(
        core.reshape(1),
        inside,
        *planes,
        *fetched[3:],
        in_hbm(elec_field),
        in_hbm(adjoint),
        in_hbm(temp_grad),
        in_hbm(adjoint_grad),
    )
    last_dense, mine, other = pl.pallas_call(
        rim_kernel,
        out_shape=(shape((fine_x, 8, fine_z), jnp.float32), half, half),
        in_specs=[in_smem] * 2 + [in_vmem] * len(handed),
        out_specs=(in_vmem,) * 3,
        scratch_shapes=(
            pltpu.VMEM((112, LANES), jnp.float32),
            pltpu.VMEM((192, 256), jnp.float32),
            pltpu.VMEM((WINDOW, LANES), jnp.float32),
            pltpu.VMEM((2, 3, 64, LANES), jnp.bfloat16),
        )
        + group_scratch(1),
        compiler_params=pltpu.CompilerParams(vmem_limit_bytes=16 * MIB),
        cost_estimate=pl.CostEstimate(
            flops=400000000, bytes_accessed=2000000, transcendentals=400000
        ),
        name="rim",
    )(part, inside, rim, *held_back)
    density = jnp.concatenate([most, last_dense], 1)
    grad_three, grad_four = sum_everywhere(mine, other, part)
    return (density, grad_three, grad_four)


def solution(mesh):
    return jax.shard_map(
        shards,
        mesh=mesh,
        in_specs=(
            P(None, None, "gy", None),
            P(),
            P(),
            P(None, "gx", "gy", None),
            P(None, "gx", "gy", None),
            P("gx", "gy", None),
            P(None, "gx", "gy", None),
        ),
        out_specs=(P("gx", "gy", None), P(), P()),
        check_vma=False,
    )
```
